32 devices in a mesh: text: 2 (over core), tag: 16 (over z, y, x).
Axes of the slice: x: 2, y: 2, z: 4, core: 2. Of those that a mesh axis runs over, the one named last changes fastest.
Arguments:
- tile_values: bfloat16 [2, 160, 512, 512], P('text', 'tag'), may hold values from -0.1875 to 0.1875
- tile_rows: int32 [2, 160], P('text', 'tag'), may hold values from 0 to 3, as said below
- tile_cols: int32 [2, 160], P('text', 'tag'), may hold values from 0 to 2, as said below
- tile_counts: int32 [2, 16], P('text', 'tag'), may hold values from 1 to 10, as said below
- panel_init: bfloat16 [4096, 512], P(('text', 'tag')), may hold values from -6 to 6
Outputs:
- text_white: float32 [4096, 512], P(('text', 'tag'))
- tag_white: float32 [24576, 512], P(('tag', 'text'))
The draws below stay inside these ranges and needn't reach their ends.
Inputs may be any that keep to these rules, and one draw needn't show every extreme that they name: `tile_rows`: within one pair of blocks the live slots name distinct tile positions. `tile_cols`: within one pair of blocks the live slots name distinct tile positions. `tile_counts`: in every draw some pair of blocks holds exactly 10 tiles.
All inputs are finite; a program needn't handle non-finite values.
Results may differ from the reference program's by a relative error of at most 0.005.
Values may be sent and summed in bfloat16 or wider, within the bound.
A program may use at most 64 MiB of HBM per device.

```python
import jax
import jax.numpy as jnp
from jax import lax

TILE = 512
K = 512
TR = 4
TC = 3
SLOTS = 10
ITERS = 1
TEXT_DEVS = 2
TAG_DEVS = 16
NR = 4096
NC = 24576
N_TEXT = 2
N_TAG = 16


def pattern(key):
    devices = TEXT_DEVS * TAG_DEVS
    pattern_key = jax.random.fold_in(key, 7)
    device_keys = jax.random.split(pattern_key, devices)
    positions = jax.vmap(lambda one_key: jax.random.permutation(one_key, TR * TC))(device_keys)[:, :SLOTS]
    lowest = max(SLOTS // 2, 1)
    counts = jax.random.randint(jax.random.fold_in(key, 11), (devices,), lowest, SLOTS + 1)
    full_device = jax.random.randint(jax.random.fold_in(key, 13), (), 0, devices)
    counts = jnp.where(jnp.arange(devices) == full_device, SLOTS, counts)
    return (positions.astype(jnp.int32), counts.astype(jnp.int32))


def draw_tile_rows(key, part):
    positions, counts = pattern(key)
    return (positions // TC).reshape(TEXT_DEVS, TAG_DEVS * SLOTS).astype(jnp.int32)


def draw_tile_cols(key, part):
    positions, counts = pattern(key)
    return (positions % TC).reshape(TEXT_DEVS, TAG_DEVS * SLOTS).astype(jnp.int32)


def draw_tile_counts(key, part):
    positions, counts = pattern(key)
    return counts.reshape(TEXT_DEVS, TAG_DEVS).astype(jnp.int32)


def block_levels(rng, shape, pieces, least, top_value):
    def one(axis_at, parts):
        heights = jax.random.uniform(jax.random.fold_in(jax.random.fold_in(rng, 6), axis_at), (parts,), jnp.float32, least / len(pieces), top_value / len(pieces))
        return jnp.repeat(jnp.exp(heights), shape[axis_at] // parts).reshape((-1,) + (1,) * (len(shape) - axis_at - 1))

    loudness = one(*pieces[0])
    for cut in pieces[1:]:
        loudness = loudness * one(*cut)
    return loudness


def gaussian(rng, extent, width, limit, cuts=(), kind=jnp.bfloat16):
    array = jax.random.normal(rng, extent, jnp.float32) * width
    if len(cuts) > 0:
        array = block_levels(rng, extent, cuts, -0.22, 0.18) * array
    return jnp.clip(array, min=-limit, max=limit).astype(kind)


def setup_inputs(seed: int = 0) -> dict:
    key_of = jax.random.split(jax.random.key(seed), 6)
    tile_values = gaussian(key_of[0], (N_TEXT, N_TAG * SLOTS, TILE, TILE), (TILE * N_TEXT) ** -0.5, 0.1875, ((0, 2), (1, 16)))
    tile_rows = draw_tile_rows(jax.random.fold_in(key_of[5], 71), 0)
    tile_cols = draw_tile_cols(jax.random.fold_in(key_of[5], 71), 0)
    tile_counts = draw_tile_counts(jax.random.fold_in(key_of[5], 71), 0)
    panel_init = gaussian(key_of[4], (NR, K), 1.0, 6.0, ((0, 32),))
    return {"tile_values": tile_values, "tile_rows": tile_rows, "tile_cols": tile_cols, "tile_counts": tile_counts, "panel_init": panel_init}


def whiten(panel, total_rows):
    gram_rows = lax.dot_general(panel.astype(jnp.float32), panel.astype(jnp.float32), (((0,), (0,)), ((), ())), preferred_element_type=jnp.float32)
    factor = jnp.linalg.cholesky(gram_rows)
    solved = lax.linalg.triangular_solve(factor, panel.astype(jnp.float32), left_side=False, lower=True, transpose_a=True)
    return solved * jnp.sqrt(jnp.float32(total_rows))

def reference(tile_values, tile_rows, tile_cols, tile_counts, panel_init):
    total_tiles = TEXT_DEVS * TAG_DEVS * SLOTS
    flat_tiles = tile_values.reshape(total_tiles, TILE, TILE)
    order = jnp.arange(total_tiles, dtype=jnp.int32)
    text_index = order // (TAG_DEVS * SLOTS)
    tag_index = order // SLOTS % TAG_DEVS
    slot_index = order % SLOTS
    counts_flat = tile_counts.reshape(-1).astype(jnp.int32)
    is_live = slot_index < counts_flat[order // SLOTS]
    row_tile = (text_index * TR + tile_rows.reshape(-1)).astype(jnp.int32)
    col_tile = (tag_index * TC + tile_cols.reshape(-1)).astype(jnp.int32)
    text_panel = panel_init
    tag_panel = jnp.zeros((NC, K), jnp.bfloat16)
    for step in range(ITERS):

        def add_tag(totals, slot_items):
            tile_block, row_at, col_at, live_flag = slot_items

            def accumulate(current):
                source = lax.dynamic_slice_in_dim(text_panel, row_at * TILE, TILE, 0)
                update = lax.dot_general(tile_block.astype(jnp.float32), source.astype(jnp.float32), (((0,), (0,)), ((), ())), preferred_element_type=jnp.float32)
                before = lax.dynamic_slice_in_dim(current, col_at * TILE, TILE, 0)
                return lax.dynamic_update_slice_in_dim(current, before + update, col_at * TILE, 0)
            return (lax.cond(live_flag, accumulate, lambda current: current, totals), None)
        tag_sums, _ = lax.scan(add_tag, jnp.zeros((NC, K), jnp.float32), (flat_tiles, row_tile, col_tile, is_live))
        tag_panel = tag_sums.astype(jnp.bfloat16)

        def add_text(totals, slot_items):
            tile_block, row_at, col_at, live_flag = slot_items

            def accumulate(current):
                source = lax.dynamic_slice_in_dim(tag_panel, col_at * TILE, TILE, 0)
                update = jnp.dot(tile_block.astype(jnp.float32), source.astype(jnp.float32), preferred_element_type=jnp.float32)
                before = lax.dynamic_slice_in_dim(current, row_at * TILE, TILE, 0)
                return lax.dynamic_update_slice_in_dim(current, before + update, row_at * TILE, 0)
            return (lax.cond(live_flag, accumulate, lambda current: current, totals), None)
        text_sums, _ = lax.scan(add_text, jnp.zeros((NR, K), jnp.float32), (flat_tiles, row_tile, col_tile, is_live))
        text_panel = text_sums.astype(jnp.bfloat16)
    return (whiten(text_panel, NR), whiten(tag_panel, NC))
```

```python
import functools
import math

import jax
import jax.numpy as jnp
from jax import lax
from jax.experimental import pallas as pl
from jax.experimental.pallas import tpu as pltpu
from jax.sharding import PartitionSpec as P

TC = 3
LANES = 128
VMEM = pltpu.VMEM


def tag_kernel(rows, cols, count, tile, panel, out):
    slot = pl.program_id(0)
    width = tile.shape[1]

    @pl.when(slot == 0)
    def _():
        out[...] = jnp.zeros_like(out)

    @pl.when(slot < count[0])
    def _():
        source = panel[pl.ds(pl.multiple_of(rows[slot] * width, width), width), :]
        into = pl.ds(pl.multiple_of(cols[slot] * width, width), width)
        out[into, :] += lax.dot_general(
            tile[0], source, (((0,), (0,)), ((), ())), preferred_element_type=jnp.float32
        )


def text_kernel(rows, cols, count, tile, panel, out, total):
    slot = pl.program_id(0)
    width = tile.shape[1]

    @pl.when(slot == 0)
    def _():
        total[...] = jnp.zeros_like(total)

    @pl.when(slot < count[0])
    def _():
        source = panel[pl.ds(pl.multiple_of(cols[slot] * width, width), width), :]
        into = pl.ds(pl.multiple_of(rows[slot] * width, width), width)
        total[into, :] += jnp.dot(tile[0], source, preferred_element_type=jnp.float32)

    @pl.when(slot == pl.num_programs(0) - 1)
    def _():
        out[...] = total[...].astype(out.dtype)


def tile_product(kernel, tiles, rows, cols, count, panel, out_rows, out_type, scratch):
    slots, width, _ = tiles.shape
    comps = panel.shape[1]

    def tile_at(slot, rows, cols, count):
        return (jnp.minimum(slot, count[0] - 1), 0, 0)

    def whole(slot, rows, cols, count):
        return (0, 0)

    return pl.pallas_call(
        kernel,
        out_shape=jax.ShapeDtypeStruct((out_rows, comps), out_type),
        grid_spec=pltpu.PrefetchScalarGridSpec(
            num_scalar_prefetch=3,
            grid=(slots,),
            in_specs=[
                pl.BlockSpec((1, width, width), tile_at),
                pl.BlockSpec(panel.shape, whole),
            ],
            out_specs=pl.BlockSpec((out_rows, comps), whole),
            scratch_shapes=scratch,
        ),
        compiler_params=pltpu.CompilerParams(vmem_limit_bytes=20 << 20),
    )(rows, cols, count, tiles, panel)


def eliminate(block):
    size = block.shape[0]
    groups = size // 8
    lane = lax.broadcasted_iota(jnp.int32, (8, size), 1)
    sub = lax.broadcasted_iota(jnp.int32, (8, size), 0)
    fixed = [jnp.full((8, size), s, jnp.int32) for s in range(8)]
    m = [block[8 * g : 8 * g + 8, :] for g in range(groups)]
    pivots = []

    def across(rows, k):
        return jnp.broadcast_to(rows[:, k : k + 1], (8, size))

    def down(rows, s):
        return jnp.broadcast_to(rows[s : s + 1, :], (8, size))

    def splat(rows, s):
        return jnp.take_along_axis(rows, fixed[s], axis=0, mode="promise_in_bounds")

    for g in range(groups):
        at = 8 * g
        inside = (lane >= at) & (lane < at + 8)
        own = [across(m[g], at + t) for t in range(8)]
        entry = {(s, t): splat(own[t], s) for t in range(8) for s in range(t, 8)}
        start = jnp.where(inside, jnp.where(lane == sub + at, 1.0, 0.0), m[g])
        rows = [down(start, s) for s in range(8)]
        pivot, steps = [None] * 8, []
        for t in range(0, 8, 2):
            a, b, c = entry[t, t], entry[t + 1, t], entry[t + 1, t + 1]
            det = a * c - b * b
            inverse, first = 1.0 / det, 1.0 / a
            later = range(t + 2, 8)
            left = {q: c * entry[q, t] - b * entry[q, t + 1] for q in later}
            right = {q: a * entry[q, t + 1] - b * entry[q, t] for q in later}
            for q in later:
                for s in range(q, 8):
                    taken = left[q] * entry[s, t] + right[q] * entry[s, t + 1]
                    entry[s, q] = entry[s, q] - inverse * taken
            left = {q: inverse * left[q] for q in later}
            right = {q: inverse * right[q] for q in later}
            upper, under = rows[t], rows[t + 1]
            for q in later:
                rows[q] = rows[q] - (left[q] * upper + right[q] * under)
            steps.append(
                (left, right, inverse * (c * upper - b * under), inverse * (a * under - b * upper))
            )
            rows[t + 1] = under - (b * first) * upper
            pivot[t], pivot[t + 1] = a, det * first
        for i in range(g + 1, groups):
            columns = [across(m[i], at + t) for t in range(8)]
            total = jnp.where(inside, 0.0, m[i])
            for t in range(0, 8, 2):
                left, right, upper, under = steps[t // 2]
                for q in range(t + 2, 8):
                    taken = left[q] * columns[t] + right[q] * columns[t + 1]
                    columns[q] = columns[q] - taken
                total = total - (columns[t] * upper + columns[t + 1] * under)
            m[i] = total
        done, kept = rows[0], pivot[0]
        for t in range(1, 8):
            done = jnp.where(sub == t, rows[t], done)
            kept = jnp.where(sub == t, pivot[t], kept)
        m[g] = done
        pivots.append(kept)
    out = []
    for g in range(groups):
        kept = jnp.where(lane <= sub + 8 * g, m[g], 0.0)
        out.append(kept * lax.rsqrt(pivots[g]))
    return jnp.concatenate(out, axis=0)


def factor_in_place(work, scale, out):
    size = work.shape[0]
    blocks = size // LANES
    exact = lax.Precision.HIGHEST
    lane = lax.broadcasted_iota(jnp.int32, (LANES, LANES), 1)
    sub = lax.broadcasted_iota(jnp.int32, (LANES, LANES), 0)
    tall = []
    for b in range(blocks):
        lo, hi = b * LANES, (b + 1) * LANES
        diagonal = jnp.where(lane == sub, work[lo:hi, lo:hi], 0.0)
        scale[:, lo:hi] = lax.rsqrt(jnp.sum(diagonal, axis=0, keepdims=True))
        tall.append(lax.rsqrt(jnp.sum(diagonal, axis=1, keepdims=True)))
    for b in range(blocks):
        lo, hi = b * LANES, (b + 1) * LANES
        work[lo:hi, :] = (work[lo:hi, :] * tall[b]) * scale[...]

    for b in range(blocks):
        lo, hi = b * LANES, (b + 1) * LANES
        inverse = eliminate(work[lo:hi, lo:hi])
        row = jnp.dot(
            inverse, work[lo:hi, :], preferred_element_type=jnp.float32, precision=exact
        )
        work[lo:hi, :] = row
        work[lo:hi, lo:hi] = inverse
        if hi < size:
            work[hi:, lo:hi] = jnp.zeros((size - hi, LANES), jnp.float32)
            work[hi:, :] -= lax.dot_general(
                work[lo:hi, hi:],
                work[lo:hi, :],
                (((0,), (0,)), ((), ())),
                preferred_element_type=jnp.float32,
                precision=exact,
            )
        lanes = lax.broadcasted_iota(jnp.int32, (LANES, size), 1)
        subs = lax.broadcasted_iota(jnp.int32, (LANES, size), 0) + lo
        out[lo:hi, :] = jnp.where(lanes <= subs, work[lo:hi, :] * scale[...], 0.0)


def factor_kernel(gram, out, work, scale):
    work[...] = gram[...]
    factor_in_place(work, scale, out)


def inverse_factor(gram):
    return pl.pallas_call(
        factor_kernel,
        out_shape=jax.ShapeDtypeStruct(gram.shape, jnp.float32),
        in_specs=[pl.BlockSpec(memory_space=VMEM)],
        out_specs=pl.BlockSpec(memory_space=VMEM),
        scratch_shapes=[VMEM(gram.shape, jnp.float32), VMEM((1, gram.shape[1]), jnp.float32)],
        compiler_params=pltpu.CompilerParams(vmem_limit_bytes=16 << 20),
    )(gram)


def white_kernel(text_scale, tag_scale, text, tag, inverses, text_out, tag_out):
    for panel, kind, out, scale in ((text, 0, text_out, text_scale), (tag, 1, tag_out, tag_scale)):
        whole = inverses[kind] * scale
        high = whole.astype(jnp.bfloat16)
        low = (whole - high.astype(jnp.float32)).astype(jnp.bfloat16)
        rows = panel.shape[0]
        step = min(rows, LANES)
        for at in range(0, rows, step):
            part = panel[at : at + step, :]
            dims = (((1,), (1,)), ((), ()))
            out[at : at + step, :] = lax.dot_general(
                part, high, dims, preferred_element_type=jnp.float32
            ) + lax.dot_general(part, low, dims, preferred_element_type=jnp.float32)


def whiten(text, tag, inverses, text_scale, tag_scale):
    return pl.pallas_call(
        functools.partial(white_kernel, text_scale, tag_scale),
        out_shape=(
            jax.ShapeDtypeStruct(text.shape, jnp.float32),
            jax.ShapeDtypeStruct(tag.shape, jnp.float32),
        ),
        in_specs=[pl.BlockSpec(memory_space=VMEM)] * 3,
        out_specs=[pl.BlockSpec(memory_space=VMEM)] * 2,
        compiler_params=pltpu.CompilerParams(vmem_limit_bytes=16 << 20),
    )(text, tag, inverses)


def local_gram(panel):
    return lax.dot_general(
        panel, panel, (((0,), (0,)), ((), ())), preferred_element_type=jnp.float32
    )


MESH = pl.DeviceIdType.MESH


def flip(me, offset):
    total, bit = me, 1
    while bit <= offset:
        if offset & bit:
            total = total + bit * (1 - 2 * lax.rem(lax.div(me, bit), 2))
        bit *= 2
    return total


def hypercube(size, rows, unit):
    bits = size.bit_length() - 1
    down = tuple(reversed(range(bits)))
    orders = [down]
    if bits >= 3:
        orders += [down[:-2] + (down[-1], down[-2]), (0, 1) + down[:-2]]
    units = rows // unit
    pieces, at = [], 0
    for number, order in enumerate(orders):
        here = units // len(orders) + (1 if number < units % len(orders) else 0)
        if here:
            pieces.append((order, at * unit, (at + here) * unit))
            at += here
    return pieces


def arrivals(order, stage):
    found = [1 << order[stage]]
    for bit in order[:stage]:
        found += [offset | 1 << bit for offset in found]
    return found


def greet(groups):
    barrier = pltpu.get_barrier_semaphore()
    for device in groups:
        pl.semaphore_signal(barrier, inc=1, device_id=device, device_id_type=MESH)
    pl.semaphore_wait(barrier, len(groups))


def tag_partners(size):
    me = lax.axis_index("tag")
    return [{"tag": flip(me, 1 << bit)} for bit in range(size.bit_length() - 1)]


def spread(pieces, source, place, send, recv):
    me = lax.axis_index("tag")
    copies = {}

    def go(number, offset, bit):
        order, lo, hi = pieces[number]
        owner = flip(me, offset)
        to = offset | 1 << bit
        copies[number, to] = pltpu.make_async_remote_copy(
            src_ref=source(lo, hi) if offset == 0 else place(owner, lo, hi),
            dst_ref=place(owner, lo, hi),
            send_sem=send.at[number, to],
            recv_sem=recv.at[number, to],
            device_id={"tag": flip(me, 1 << bit)},
            device_id_type=MESH,
        )
        copies[number, to].start()

    bits = len(pieces[0][0])
    for stage in range(bits):
        for number, (order, _, _) in enumerate(pieces):
            go(number, 0, order[stage])
    for stage in range(bits):
        for turn in range(1 << stage):
            for number, (order, _, _) in enumerate(pieces):
                offset = arrivals(order, stage)[turn]
                copies[number, offset].wait_recv()
                for later in range(stage + 1, bits):
                    go(number, offset, order[later])
    return copies


def collect_start(pieces, source, land, send, recv):
    me = lax.axis_index("tag")
    copies = {}
    last = len(pieces[0][0]) - 1
    for turn in range(1 << last):
        for number, (order, lo, hi) in enumerate(pieces):
            offset = arrivals(order, last)[turn]
            copies[number, offset] = pltpu.make_async_remote_copy(
                src_ref=source(flip(me, offset), lo, hi),
                dst_ref=land.at[offset, lo:hi],
                send_sem=send.at[number, offset],
                recv_sem=recv.at[number, offset],
                device_id={"tag": flip(me, 1 << order[last])},
                device_id_type=MESH,
            )
            copies[number, offset].start()
    return copies


def collect(pieces, copies, source, land, outgoing, finish, send, recv):
    me = lax.axis_index("tag")
    bits = len(pieces[0][0])

    def summed(number, offset, stage):
        order, lo, hi = pieces[number]
        total = source(flip(me, offset), lo, hi)[...].astype(jnp.float32)
        for later in reversed(range(stage + 1, bits)):
            come = offset | 1 << order[later]
            copies[number, come].wait_recv()
            total = total + land[come, lo:hi].astype(jnp.float32)
        return total

    for stage in reversed(range(bits - 1)):
        for turn in range(1 << stage):
            for number, (order, lo, hi) in enumerate(pieces):
                offset = arrivals(order, stage)[turn]
                outgoing[offset, lo:hi] = summed(number, offset, stage).astype(outgoing.dtype)
                copies[number, offset] = pltpu.make_async_remote_copy(
                    src_ref=outgoing.at[offset, lo:hi],
                    dst_ref=land.at[offset, lo:hi],
                    send_sem=send.at[number, offset],
                    recv_sem=recv.at[number, offset],
                    device_id={"tag": flip(me, 1 << order[stage])},
                    device_id_type=MESH,
                )
                copies[number, offset].start()
    for number, (_, lo, hi) in enumerate(pieces):
        finish(lo, hi, summed(number, 0, -1))


def drain(copies):
    for copy in copies.values():
        copy.wait_send()


def gather_kernel(size, pieces, shard, out, send, recv):
    rows = shard.shape[0]
    greet(tag_partners(size))

    def place(owner, lo, hi):
        return out.at[pl.ds(pl.multiple_of(owner * rows + lo, 16), hi - lo), :]

    copies = spread(pieces, lambda lo, hi: shard.at[lo:hi, :], place, send, recv)
    me = lax.axis_index("tag")
    out[pl.ds(pl.multiple_of(me * rows, 16), rows), :] = shard[...]
    drain(copies)


def remote_call(kernel, number, out_shape, scratch, count):
    many = isinstance(out_shape, tuple)
    spec = pl.BlockSpec(memory_space=VMEM)
    return pl.pallas_call(
        kernel,
        out_shape=out_shape,
        in_specs=[spec] * count,
        out_specs=[spec] * len(out_shape) if many else spec,
        scratch_shapes=scratch,
        cost_estimate=pl.CostEstimate(flops=0, bytes_accessed=50_000_000, transcendentals=0),
        compiler_params=pltpu.CompilerParams(
            collective_id=number, has_side_effects=True, vmem_limit_bytes=20 << 20
        ),
    )


def semaphores(*shape):
    return pltpu.SemaphoreType.DMA(shape)


def gather(shard, size):
    rows, comps = shard.shape
    pieces = hypercube(size, rows, 16)
    return remote_call(
        functools.partial(gather_kernel, size, pieces),
        0,
        jax.ShapeDtypeStruct((rows * size, comps), shard.dtype),
        [semaphores(len(pieces), size), semaphores(len(pieces), size)],
        1,
    )(shard)


def pair_sum_kernel(chunk, partial, out, mine, land, leaving, send, recv):
    core = lax.axis_index("text")
    sibling = {"text": 1 - core}
    half = mine.shape[0]
    greet([sibling])
    first, second = [], []
    for number in range(half // chunk):
        lo = number * chunk
        theirs = pl.multiple_of((1 - core) * half + lo, 16)
        leaving[lo : lo + chunk, :] = partial[pl.ds(theirs, chunk), :].astype(leaving.dtype)
        copy = pltpu.make_async_remote_copy(
            src_ref=leaving.at[lo : lo + chunk, :],
            dst_ref=land.at[lo : lo + chunk, :],
            send_sem=send.at[0, number],
            recv_sem=recv.at[0, number],
            device_id=sibling,
            device_id_type=MESH,
        )
        copy.start()
        first.append(copy)
    for number in range(half // chunk):
        lo = number * chunk
        ours = pl.ds(pl.multiple_of(core * half + lo, 16), chunk)
        first[number].wait_recv()
        total = (partial[ours, :] + land[lo : lo + chunk, :].astype(jnp.float32)).astype(out.dtype)
        mine[lo : lo + chunk, :] = total
        copy = pltpu.make_async_remote_copy(
            src_ref=mine.at[lo : lo + chunk, :],
            dst_ref=out.at[ours, :],
            send_sem=send.at[1, number],
            recv_sem=recv.at[1, number],
            device_id=sibling,
            device_id_type=MESH,
        )
        copy.start()
        second.append(copy)
        out[ours, :] = total
    for copy in first:
        copy.wait_send()
    for copy in second:
        copy.wait()


def pair_sum(partial):
    rows, comps = partial.shape
    half = rows // 2
    chunk = half // 6
    return remote_call(
        functools.partial(pair_sum_kernel, chunk),
        1,
        (
            jax.ShapeDtypeStruct((rows, comps), jnp.bfloat16),
            jax.ShapeDtypeStruct((half, comps), jnp.bfloat16),
        ),
        [
            VMEM((half, comps), jnp.bfloat16),
            VMEM((half, comps), jnp.bfloat16),
            semaphores(2, 6),
            semaphores(2, 6),
        ],
        1,
    )(partial)


def scatter_kernel(size, pieces, partial, out, land, outgoing, send, recv):
    rows = out.shape[0]
    greet(tag_partners(size))

    def source(owner, lo, hi):
        return partial.at[pl.ds(pl.multiple_of(owner * rows + lo, 16), hi - lo), :]

    def finish(lo, hi, total):
        out[lo:hi, :] = total.astype(out.dtype)

    copies = collect_start(pieces, source, land, send, recv)
    collect(pieces, copies, source, land, outgoing, finish, send, recv)
    drain(copies)


def scatter_sum(partial, size):
    rows, comps = partial.shape[0] // size, partial.shape[1]
    pieces = hypercube(size, rows, 16)
    return remote_call(
        functools.partial(scatter_kernel, size, pieces),
        2,
        jax.ShapeDtypeStruct((rows, comps), jnp.bfloat16),
        [
            VMEM((size, rows, comps), jnp.bfloat16),
            VMEM((size, rows, comps), jnp.bfloat16),
            semaphores(len(pieces), size),
            semaphores(len(pieces), size),
        ],
        1,
    )(partial)


def lower(blocks):
    return [(i, j) for i in range(blocks) for j in range(i + 1)]


def gram_kernel(size, pieces, text, tag, out, both, other, own, gathered, land, outgoing, pair, sems):
    core = lax.axis_index("text")
    me = lax.axis_index("tag")
    rows = own.shape[1]
    pairs = lower(out.shape[0] // LANES)
    sibling = {"text": 1 - core}
    greet(tag_partners(size) + [sibling])
    for kind, panel in ((0, text), (1, tag)):
        gram = local_gram(panel[...])
        for at, (i, j) in enumerate(pairs):
            both[kind, at] = gram[i * LANES : (i + 1) * LANES, j * LANES : (j + 1) * LANES]
    swap = pltpu.make_async_remote_copy(
        src_ref=both.at[1 - core],
        dst_ref=other,
        send_sem=pair.at[0],
        recv_sem=pair.at[1],
        device_id=sibling,
        device_id_type=MESH,
    )
    swap.start()
    swap.wait()
    other[...] += both[core]

    def place(owner, lo, hi):
        return gathered.at[lo:hi, pl.ds(pl.multiple_of(owner * rows, 8), rows), :]

    def source(owner, lo, hi):
        return other.at[lo:hi, pl.ds(pl.multiple_of(owner * rows, 8), rows), :]

    def finish(lo, hi, total):
        own[lo:hi] = total

    copies = collect_start(pieces, source, land, sems.at[0], sems.at[1])
    collect(pieces, copies, source, land, outgoing, finish, sems.at[0], sems.at[1])
    more = spread(pieces, lambda lo, hi: own.at[lo:hi], place, sems.at[2], sems.at[3])
    gathered[:, pl.ds(pl.multiple_of(me * rows, 8), rows), :] = own[...]
    drain(copies)
    drain(more)
    for at, (i, j) in enumerate(pairs):
        block = gathered[at]
        if i == j:
            out[i * LANES : (i + 1) * LANES, j * LANES : (j + 1) * LANES] = block
        else:
            out[j * LANES : (j + 1) * LANES, i * LANES : (i + 1) * LANES] = block.T
            out[i * LANES : (i + 1) * LANES, j * LANES : (j + 1) * LANES] = block


def gram_sum(text, tag, size):
    comps = text.shape[1]
    rows = LANES // size
    count = len(lower(comps // LANES))
    pieces = hypercube(size, count, 1)
    square = jax.ShapeDtypeStruct((comps, comps), jnp.float32)
    return remote_call(
        functools.partial(gram_kernel, size, pieces),
        3,
        square,
        [
            VMEM((2, count, LANES, LANES), jnp.float32),
            VMEM((count, LANES, LANES), jnp.float32),
            VMEM((count, rows, LANES), jnp.float32),
            VMEM((count, LANES, LANES), jnp.float32),
            VMEM((size, count, rows, LANES), jnp.float32),
            VMEM((size, count, rows, LANES), jnp.float32),
            semaphores(2),
            semaphores(4, len(pieces), size),
        ],
        2,
    )(text, tag)


def swap_kernel(inverse, out, sems):
    core = lax.axis_index("text")
    sibling = {"text": 1 - core}
    greet([sibling])
    swap = pltpu.make_async_remote_copy(
        src_ref=inverse,
        dst_ref=out.at[core],
        send_sem=sems.at[0],
        recv_sem=sems.at[1],
        device_id=sibling,
        device_id_type=MESH,
    )
    swap.start()
    out[core] = inverse[...]
    swap.wait()


def swap_inverses(inverse):
    return remote_call(
        swap_kernel,
        4,
        jax.ShapeDtypeStruct((2,) + inverse.shape, jnp.float32),
        [semaphores(2)],
        1,
    )(inverse)


def shards(tile_values, tile_rows, tile_cols, tile_counts, panel_init):
    tiles = tile_values[0]
    rows = tile_rows[0]
    cols = tile_cols[0]
    count = tile_counts[0]
    width = tiles.shape[1]
    comps = panel_init.shape[1]
    text_size = lax.axis_size("text")
    tag_size = lax.axis_size("tag")
    column_span = TC * width
    share = column_span // text_size
    paired = text_size == 2 and LANES // tag_size >= 8
    row_block = gather(panel_init, tag_size)
    row_span = row_block.shape[0]

    tag_partial = tile_product(
        tag_kernel, tiles, rows, cols, count, row_block, column_span, jnp.float32, []
    )
    if paired:
        column_block, tag_mine = pair_sum(tag_partial)
    else:
        column_block = lax.psum(tag_partial, "text").astype(jnp.bfloat16)
        tag_mine = lax.dynamic_slice_in_dim(
            column_block, lax.axis_index("text") * share, share, 0
        )
    text_partial = tile_product(
        text_kernel,
        tiles,
        rows,
        cols,
        count,
        column_block,
        row_span,
        jnp.bfloat16,
        [VMEM((row_span, comps), jnp.float32)],
    )
    text_mine = scatter_sum(text_partial, tag_size)
    if paired:
        gram = gram_sum(text_mine, tag_mine, tag_size)
        inverses = swap_inverses(inverse_factor(gram))
    else:
        text_gram, tag_gram = lax.psum(
            (local_gram(text_mine), local_gram(tag_mine)), ("text", "tag")
        )
        inverses = jnp.stack([inverse_factor(text_gram), inverse_factor(tag_gram)])
    text_total = text_mine.shape[0] * tag_size * text_size
    tag_total = column_span * tag_size
    return whiten(text_mine, tag_mine, inverses, math.sqrt(text_total), math.sqrt(tag_total))


def solution(mesh):
    in_specs = (
        P("text", "tag", None, None),
        P("text", "tag"),
        P("text", "tag"),
        P("text", "tag"),
        P(("text", "tag"), None),
    )
    out_specs = (P(("text", "tag"), None), P(("tag", "text"), None))
    return jax.shard_map(shards, mesh=mesh, in_specs=in_specs, out_specs=out_specs, check_vma=False)
```

```python
import functools
import math

import jax
import jax.numpy as jnp
from jax import lax
from jax.experimental import pallas as pl
from jax.experimental.pallas import tpu as pltpu
from jax.sharding import PartitionSpec as P

TC = 3
LANES = 128
VMEM = pltpu.VMEM


def tag_kernel(rows, cols, count, tile, panel, out):
    slot = pl.program_id(0)
    width = tile.shape[1]

    @pl.when(slot == 0)
    def _():
        out[...] = jnp.zeros_like(out)

    @pl.when(slot < count[0])
    def _():
        source = panel[pl.ds(pl.multiple_of(rows[slot] * width, width), width), :]
        into = pl.ds(pl.multiple_of(cols[slot] * width, width), width)
        out[into, :] += lax.dot_general(
            tile[0], source, (((0,), (0,)), ((), ())), preferred_element_type=jnp.float32
        )


def text_kernel(rows, cols, count, tile, panel, out, total):
    slot = pl.program_id(0)
    width = tile.shape[1]

    @pl.when(slot == 0)
    def _():
        total[...] = jnp.zeros_like(total)

    @pl.when(slot < count[0])
    def _():
        source = panel[pl.ds(pl.multiple_of(cols[slot] * width, width), width), :]
        into = pl.ds(pl.multiple_of(rows[slot] * width, width), width)
        total[into, :] += jnp.dot(tile[0], source, preferred_element_type=jnp.float32)

    @pl.when(slot == pl.num_programs(0) - 1)
    def _():
        out[...] = total[...].astype(out.dtype)


def tile_product(kernel, tiles, rows, cols, count, panel, out_rows, out_type, scratch):
    slots, width, _ = tiles.shape
    comps = panel.shape[1]

    def tile_at(slot, rows, cols, count):
        return (jnp.minimum(slot, count[0] - 1), 0, 0)

    def whole(slot, rows, cols, count):
        return (0, 0)

    return pl.pallas_call(
        kernel,
        out_shape=jax.ShapeDtypeStruct((out_rows, comps), out_type),
        grid_spec=pltpu.PrefetchScalarGridSpec(
            num_scalar_prefetch=3,
            grid=(slots,),
            in_specs=[
                pl.BlockSpec((1, width, width), tile_at),
                pl.BlockSpec(panel.shape, whole),
            ],
            out_specs=pl.BlockSpec((out_rows, comps), whole),
            scratch_shapes=scratch,
        ),
        compiler_params=pltpu.CompilerParams(vmem_limit_bytes=20 << 20),
    )(rows, cols, count, tiles, panel)


def eliminate(block):
    size = block.shape[0]
    groups = size // 8
    lane = lax.broadcasted_iota(jnp.int32, (8, size), 1)
    sub = lax.broadcasted_iota(jnp.int32, (8, size), 0)
    fixed = [jnp.full((8, size), s, jnp.int32) for s in range(8)]
    m = [block[8 * g : 8 * g + 8, :] for g in range(groups)]
    pivots = []

    def across(rows, k):
        return jnp.broadcast_to(rows[:, k : k + 1], (8, size))

    def down(rows, s):
        return jnp.broadcast_to(rows[s : s + 1, :], (8, size))

    def splat(rows, s):
        return jnp.take_along_axis(rows, fixed[s], axis=0, mode="promise_in_bounds")

    for g in range(groups):
        at = 8 * g
        inside = (lane >= at) & (lane < at + 8)
        own = [across(m[g], at + t) for t in range(8)]
        entry = {(s, t): splat(own[t], s) for t in range(8) for s in range(t, 8)}
        start = jnp.where(inside, jnp.where(lane == sub + at, 1.0, 0.0), m[g])
        rows = [down(start, s) for s in range(8)]
        pivot, steps = [None] * 8, []
        for t in range(0, 8, 2):
            a, b, c = entry[t, t], entry[t + 1, t], entry[t + 1, t + 1]
            det = a * c - b * b
            inverse, first = 1.0 / det, 1.0 / a
            later = range(t + 2, 8)
            left = {q: c * entry[q, t] - b * entry[q, t + 1] for q in later}
            right = {q: a * entry[q, t + 1] - b * entry[q, t] for q in later}
            for q in later:
                for s in range(q, 8):
                    taken = left[q] * entry[s, t] + right[q] * entry[s, t + 1]
                    entry[s, q] = entry[s, q] - inverse * taken
            left = {q: inverse * left[q] for q in later}
            right = {q: inverse * right[q] for q in later}
            upper, under = rows[t], rows[t + 1]
            for q in later:
                rows[q] = rows[q] - (left[q] * upper + right[q] * under)
            steps.append(
                (left, right, inverse * (c * upper - b * under), inverse * (a * under - b * upper))
            )
            rows[t + 1] = under - (b * first) * upper
            pivot[t], pivot[t + 1] = a, det * first
        for i in range(g + 1, groups):
            columns = [across(m[i], at + t) for t in range(8)]
            total = jnp.where(inside, 0.0, m[i])
            for t in range(0, 8, 2):
                left, right, upper, under = steps[t // 2]
                for q in range(t + 2, 8):
                    taken = left[q] * columns[t] + right[q] * columns[t + 1]
                    columns[q] = columns[q] - taken
                total = total - (columns[t] * upper + columns[t + 1] * under)
            m[i] = total
        done, kept = rows[0], pivot[0]
        for t in range(1, 8):
            done = jnp.where(sub == t, rows[t], done)
            kept = jnp.where(sub == t, pivot[t], kept)
        m[g] = done
        pivots.append(kept)
    out = []
    for g in range(groups):
        kept = jnp.where(lane <= sub + 8 * g, m[g], 0.0)
        out.append(kept * lax.rsqrt(pivots[g]))
    return jnp.concatenate(out, axis=0)


def factor_in_place(work, scale, out):
    size = work.shape[0]
    blocks = size // LANES
    exact = lax.Precision.HIGHEST
    lane = lax.broadcasted_iota(jnp.int32, (LANES, LANES), 1)
    sub = lax.broadcasted_iota(jnp.int32, (LANES, LANES), 0)
    tall = []
    for b in range(blocks):
        lo, hi = b * LANES, (b + 1) * LANES
        diagonal = jnp.where(lane == sub, work[lo:hi, lo:hi], 0.0)
        scale[:, lo:hi] = lax.rsqrt(jnp.sum(diagonal, axis=0, keepdims=True))
        tall.append(lax.rsqrt(jnp.sum(diagonal, axis=1, keepdims=True)))
    for b in range(blocks):
        lo, hi = b * LANES, (b + 1) * LANES
        work[lo:hi, :] = (work[lo:hi, :] * tall[b]) * scale[...]

    for b in range(blocks):
        lo, hi = b * LANES, (b + 1) * LANES
        inverse = eliminate(work[lo:hi, lo:hi])
        row = jnp.dot(
            inverse, work[lo:hi, :], preferred_element_type=jnp.float32, precision=exact
        )
        work[lo:hi, :] = row
        work[lo:hi, lo:hi] = inverse
        if hi < size:
            work[hi:, lo:hi] = jnp.zeros((size - hi, LANES), jnp.float32)
            work[hi:, :] -= lax.dot_general(
                work[lo:hi, hi:],
                work[lo:hi, :],
                (((0,), (0,)), ((), ())),
                preferred_element_type=jnp.float32,
                precision=exact,
            )
        lanes = lax.broadcasted_iota(jnp.int32, (LANES, size), 1)
        subs = lax.broadcasted_iota(jnp.int32, (LANES, size), 0) + lo
        out[lo:hi, :] = jnp.where(lanes <= subs, work[lo:hi, :] * scale[...], 0.0)


def factor_kernel(gram, out, work, scale):
    work[...] = gram[...]
    factor_in_place(work, scale, out)


def inverse_factor(gram):
    return pl.pallas_call(
        factor_kernel,
        out_shape=jax.ShapeDtypeStruct(gram.shape, jnp.float32),
        in_specs=[pl.BlockSpec(memory_space=VMEM)],
        out_specs=pl.BlockSpec(memory_space=VMEM),
        scratch_shapes=[VMEM(gram.shape, jnp.float32), VMEM((1, gram.shape[1]), jnp.float32)],
        compiler_params=pltpu.CompilerParams(vmem_limit_bytes=16 << 20),
    )(gram)


def white_kernel(text_scale, tag_scale, text, tag, inverses, text_out, tag_out):
    for panel, kind, out, scale in ((text, 0, text_out, text_scale), (tag, 1, tag_out, tag_scale)):
        whole = inverses[kind] * scale
        high = whole.astype(jnp.bfloat16)
        low = (whole - high.astype(jnp.float32)).astype(jnp.bfloat16)
        rows = panel.shape[0]
        step = min(rows, LANES)
        for at in range(0, rows, step):
            part = panel[at : at + step, :]
            dims = (((1,), (1,)), ((), ()))
            out[at : at + step, :] = lax.dot_general(
                part, high, dims, preferred_element_type=jnp.float32
            ) + lax.dot_general(part, low, dims, preferred_element_type=jnp.float32)


def whiten(text, tag, inverses, text_scale, tag_scale):
    return pl.pallas_call(
        functools.partial(white_kernel, text_scale, tag_scale),
        out_shape=(
            jax.ShapeDtypeStruct(text.shape, jnp.float32),
            jax.ShapeDtypeStruct(tag.shape, jnp.float32),
        ),
        in_specs=[pl.BlockSpec(memory_space=VMEM)] * 3,
        out_specs=[pl.BlockSpec(memory_space=VMEM)] * 2,
        compiler_params=pltpu.CompilerParams(vmem_limit_bytes=16 << 20),
    )(text, tag, inverses)


def local_gram(panel):
    return lax.dot_general(
        panel, panel, (((0,), (0,)), ((), ())), preferred_element_type=jnp.float32
    )


MESH = pl.DeviceIdType.MESH


def flip(me, offset):
    total, bit = me, 1
    while bit <= offset:
        if offset & bit:
            total = total + bit * (1 - 2 * lax.rem(lax.div(me, bit), 2))
        bit *= 2
    return total


def hypercube(size, rows, unit):
    bits = size.bit_length() - 1
    down = tuple(reversed(range(bits)))
    orders = [down]
    if bits >= 3:
        orders += [down[:-2] + (down[-1], down[-2]), (0, 1) + down[:-2]]
    units = rows // unit
    pieces, at = [], 0
    for number, order in enumerate(orders):
        here = units // len(orders) + (1 if number < units % len(orders) else 0)
        if here:
            pieces.append((order, at * unit, (at + here) * unit))
            at += here
    return pieces


def arrivals(order, stage):
    found = [1 << order[stage]]
    for bit in order[:stage]:
        found += [offset | 1 << bit for offset in found]
    return found


def greet(groups):
    barrier = pltpu.get_barrier_semaphore()
    for device in groups:
        pl.semaphore_signal(barrier, inc=1, device_id=device, device_id_type=MESH)
    pl.semaphore_wait(barrier, len(groups))


def tag_partners(size):
    me = lax.axis_index("tag")
    return [{"tag": flip(me, 1 << bit)} for bit in range(size.bit_length() - 1)]


def spread(pieces, source, place, send, recv):
    me = lax.axis_index("tag")
    copies = {}

    def go(number, offset, bit):
        order, lo, hi = pieces[number]
        owner = flip(me, offset)
        to = offset | 1 << bit
        copies[number, to] = pltpu.make_async_remote_copy(
            src_ref=source(lo, hi) if offset == 0 else place(owner, lo, hi),
            dst_ref=place(owner, lo, hi),
            send_sem=send.at[number, to],
            recv_sem=recv.at[number, to],
            device_id={"tag": flip(me, 1 << bit)},
            device_id_type=MESH,
        )
        copies[number, to].start()

    bits = len(pieces[0][0])
    for stage in range(bits):
        for number, (order, _, _) in enumerate(pieces):
            go(number, 0, order[stage])
    for stage in range(bits):
        for turn in range(1 << stage):
            for number, (order, _, _) in enumerate(pieces):
                offset = arrivals(order, stage)[turn]
                copies[number, offset].wait_recv()
                for later in range(stage + 1, bits):
                    go(number, offset, order[later])
    return copies


def collect_start(pieces, source, land, send, recv):
    me = lax.axis_index("tag")
    copies = {}
    last = len(pieces[0][0]) - 1
    for turn in range(1 << last):
        for number, (order, lo, hi) in enumerate(pieces):
            offset = arrivals(order, last)[turn]
            copies[number, offset] = pltpu.make_async_remote_copy(
                src_ref=source(flip(me, offset), lo, hi),
                dst_ref=land.at[offset, lo:hi],
                send_sem=send.at[number, offset],
                recv_sem=recv.at[number, offset],
                device_id={"tag": flip(me, 1 << order[last])},
                device_id_type=MESH,
            )
            copies[number, offset].start()
    return copies


def collect(pieces, copies, source, land, outgoing, finish, send, recv):
    me = lax.axis_index("tag")
    bits = len(pieces[0][0])

    def summed(number, offset, stage):
        order, lo, hi = pieces[number]
        total = source(flip(me, offset), lo, hi)[...].astype(jnp.float32)
        for later in reversed(range(stage + 1, bits)):
            come = offset | 1 << order[later]
            copies[number, come].wait_recv()
            total = total + land[come, lo:hi].astype(jnp.float32)
        return total

    for stage in reversed(range(bits - 1)):
        for turn in range(1 << stage):
            for number, (order, lo, hi) in enumerate(pieces):
                offset = arrivals(order, stage)[turn]
                outgoing[offset, lo:hi] = summed(number, offset, stage).astype(outgoing.dtype)
                copies[number, offset] = pltpu.make_async_remote_copy(
                    src_ref=outgoing.at[offset, lo:hi],
                    dst_ref=land.at[offset, lo:hi],
                    send_sem=send.at[number, offset],
                    recv_sem=recv.at[number, offset],
                    device_id={"tag": flip(me, 1 << order[stage])},
                    device_id_type=MESH,
                )
                copies[number, offset].start()
    for number, (_, lo, hi) in enumerate(pieces):
        finish(lo, hi, summed(number, 0, -1))


def drain(copies):
    for copy in copies.values():
        copy.wait_send()


def gather_kernel(size, pieces, shard, out, send, recv):
    rows = shard.shape[0]
    greet(tag_partners(size))

    def place(owner, lo, hi):
        return out.at[pl.ds(pl.multiple_of(owner * rows + lo, 16), hi - lo), :]

    copies = spread(pieces, lambda lo, hi: shard.at[lo:hi, :], place, send, recv)
    me = lax.axis_index("tag")
    out[pl.ds(pl.multiple_of(me * rows, 16), rows), :] = shard[...]
    drain(copies)


def remote_call(kernel, number, out_shape, scratch, count):
    many = isinstance(out_shape, tuple)
    spec = pl.BlockSpec(memory_space=VMEM)
    return pl.pallas_call(
        kernel,
        out_shape=out_shape,
        in_specs=[spec] * count,
        out_specs=[spec] * len(out_shape) if many else spec,
        scratch_shapes=scratch,
        cost_estimate=pl.CostEstimate(flops=0, bytes_accessed=50_000_000, transcendentals=0),
        compiler_params=pltpu.CompilerParams(
            collective_id=number, has_side_effects=True, vmem_limit_bytes=20 << 20
        ),
    )


def semaphores(*shape):
    return pltpu.SemaphoreType.DMA(shape)


def gather(shard, size):
    rows, comps = shard.shape
    pieces = hypercube(size, rows, 16)
    return remote_call(
        functools.partial(gather_kernel, size, pieces),
        0,
        jax.ShapeDtypeStruct((rows * size, comps), shard.dtype),
        [semaphores(len(pieces), size), semaphores(len(pieces), size)],
        1,
    )(shard)


def scatter_kernel(size, pieces, partial, out, land, outgoing, send, recv):
    rows = out.shape[0]
    greet(tag_partners(size))

    def source(owner, lo, hi):
        return partial.at[pl.ds(pl.multiple_of(owner * rows + lo, 16), hi - lo), :]

    def finish(lo, hi, total):
        out[lo:hi, :] = total.astype(out.dtype)

    copies = collect_start(pieces, source, land, send, recv)
    collect(pieces, copies, source, land, outgoing, finish, send, recv)
    drain(copies)


def scatter_sum(partial, size):
    rows, comps = partial.shape[0] // size, partial.shape[1]
    pieces = hypercube(size, rows, 16)
    return remote_call(
        functools.partial(scatter_kernel, size, pieces),
        2,
        jax.ShapeDtypeStruct((rows, comps), jnp.bfloat16),
        [
            VMEM((size, rows, comps), jnp.bfloat16),
            VMEM((size, rows, comps), jnp.bfloat16),
            semaphores(len(pieces), size),
            semaphores(len(pieces), size),
        ],
        1,
    )(partial)


def spread_steps(pieces, source, place, send, recv, copies):
    me = lax.axis_index("tag")

    def go(number, offset, bit):
        order, lo, hi = pieces[number]
        owner = flip(me, offset)
        to = offset | 1 << bit
        copies[number, to] = pltpu.make_async_remote_copy(
            src_ref=source(lo, hi) if offset == 0 else place(owner, lo, hi),
            dst_ref=place(owner, lo, hi),
            send_sem=send.at[number, to],
            recv_sem=recv.at[number, to],
            device_id={"tag": flip(me, 1 << bit)},
            device_id_type=MESH,
        )
        copies[number, to].start()

    bits = len(pieces[0][0])
    for stage in range(bits):
        for number, (order, _, _) in enumerate(pieces):
            go(number, 0, order[stage])
    yield
    for stage in range(bits):
        for turn in range(1 << stage):
            for number, (order, _, _) in enumerate(pieces):
                offset = arrivals(order, stage)[turn]
                copies[number, offset].wait_recv()
                for later in range(stage + 1, bits):
                    go(number, offset, order[later])
                yield


def collect_steps(pieces, source, land, outgoing, finish, send, recv, copies):
    me = lax.axis_index("tag")
    bits = len(pieces[0][0])

    def go(number, offset, bit, ref):
        _, lo, hi = pieces[number]
        copies[number, offset] = pltpu.make_async_remote_copy(
            src_ref=ref,
            dst_ref=land(offset, lo, hi),
            send_sem=send.at[number, offset],
            recv_sem=recv.at[number, offset],
            device_id={"tag": flip(me, 1 << bit)},
            device_id_type=MESH,
        )
        copies[number, offset].start()

    def summed(number, offset, stage):
        order, lo, hi = pieces[number]
        total = source(flip(me, offset), lo, hi)[...].astype(jnp.float32)
        for later in reversed(range(stage + 1, bits)):
            come = offset | 1 << order[later]
            copies[number, come].wait_recv()
            total = total + land(come, lo, hi)[...].astype(jnp.float32)
        return total

    last = bits - 1
    for turn in reversed(range(1 << last)):
        for number, (order, lo, hi) in enumerate(pieces):
            offset = arrivals(order, last)[turn]
            go(number, offset, order[last], source(flip(me, offset), lo, hi))
    yield
    for stage in reversed(range(last)):
        for turn in reversed(range(1 << stage)):
            for number, (order, lo, hi) in enumerate(pieces):
                offset = arrivals(order, stage)[turn]
                leaving = outgoing(offset, lo, hi)
                leaving[...] = summed(number, offset, stage).astype(leaving.dtype)
                go(number, offset, order[stage], leaving)
                yield
    for number, (_, lo, hi) in enumerate(pieces):
        finish(lo, hi, summed(number, 0, -1))
        yield


def advance(steps, count):
    for _ in range(count):
        if next(steps, steps) is steps:
            return False
    return True


def finish_steps(steps):
    for _ in steps:
        pass


def weave(work, steps, lead, ratio):
    for number, _ in enumerate(work):
        if number >= lead:
            advance(steps, ratio)


def front_kernel(
    size, pieces, shard, stored, tile_rows, tile_cols, tile_counts, text_out, tag_out,
    tiles, table, panel, total, leaving, arrived, columns, partial, land, outgoing,
    tile_sem, gather_sems, pair_sems, scatter_sems,
):
    core = lax.axis_index("text")
    me = lax.axis_index("tag")
    sibling = {"text": 1 - core}
    slots, width, _ = stored.shape
    rows = shard.shape[0]
    parts, row_span, part = panel.shape
    column_span = columns.shape[1]
    row_tiles, column_tiles = row_span // width, column_span // width
    half = column_span // 2
    chunk = half // column_tiles
    load = pltpu.make_async_copy(stored, tiles.at[0:slots], tile_sem)
    load.start()
    greet(tag_partners(size) + [sibling])

    def lanes(h):
        return slice(h * part, (h + 1) * part)

    def gather(h, copies):
        def place(owner, lo, hi):
            return panel.at[h, pl.ds(pl.multiple_of(owner * rows + lo, 16), hi - lo), :]

        def source(lo, hi):
            return shard.at[lo:hi, lanes(h)]

        sems = gather_sems
        return spread_steps(pieces, source, place, sems.at[0, h], sems.at[1, h], copies)

    def scatter(h, copies):
        def source(owner, lo, hi):
            return partial.at[h, pl.ds(pl.multiple_of(owner * rows + lo, 16), hi - lo), :]

        def come(offset, lo, hi):
            return land.at[h, offset, lo:hi, :]

        def leave(offset, lo, hi):
            return outgoing.at[h, offset, lo:hi, :]

        def done(lo, hi, value):
            text_out[lo:hi, lanes(h)] = value.astype(text_out.dtype)

        sems = scatter_sems
        return collect_steps(
            pieces, source, come, leave, done, sems.at[0, h], sems.at[1, h], copies
        )

    def work(h, copies):
        def swap(phase, number, src, dst):
            copy = pltpu.make_async_remote_copy(
                src_ref=src,
                dst_ref=dst,
                send_sem=pair_sems.at[0, h, phase, number],
                recv_sem=pair_sems.at[1, h, phase, number],
                device_id=sibling,
                device_id_type=MESH,
            )
            copy.start()
            copies[phase, number] = copy

        sent = False
        for turn in range(column_tiles):
            c = core * turn + (1 - core) * (column_tiles - 1 - turn)
            into = pl.ds(pl.multiple_of(c * width, width), width)
            for r in range(row_tiles):
                product = lax.dot_general(
                    tiles[table[r * column_tiles + c]],
                    panel[h, r * width : (r + 1) * width, :],
                    (((0,), (0,)), ((), ())),
                    preferred_element_type=jnp.float32,
                )
                if r == 0:
                    total[into, :] = product
                else:
                    total[into, :] += product
                yield
            if not sent and (turn + 1) * width >= half:
                sent = True
                for number in range(column_tiles):
                    lo = number * chunk
                    theirs = pl.ds(pl.multiple_of((1 - core) * half + lo, 16), chunk)
                    leaving[h, lo : lo + chunk, :] = total[theirs, :].astype(leaving.dtype)
                    mail = leaving.at[h, lo : lo + chunk, :]
                    swap(0, number, mail, arrived.at[h, lo : lo + chunk, :])
        for number in range(column_tiles):
            lo = number * chunk
            ours = pl.ds(pl.multiple_of(core * half + lo, 16), chunk)
            copies[0, number].wait_recv()
            value = total[ours, :] + arrived[h, lo : lo + chunk, :].astype(jnp.float32)
            value = value.astype(columns.dtype)
            columns[h, ours, :] = value
            tag_out[lo : lo + chunk, lanes(h)] = value
            swap(1, number, columns.at[h, ours, :], columns.at[h, ours, :])
            yield
        for number in range(column_tiles):
            copies[1, number].wait_recv()
        for r in range(row_tiles):
            value = None
            for c in range(column_tiles):
                product = jnp.dot(
                    tiles[table[r * column_tiles + c]],
                    columns[h, c * width : (c + 1) * width, :],
                    preferred_element_type=jnp.float32,
                )
                value = product if value is None else value + product
                if c < column_tiles - 1:
                    yield
            partial[h, r * width : (r + 1) * width, :] = value.astype(partial.dtype)
            yield

    gathered, paired, summed = ([{} for _ in range(parts)] for _ in range(3))
    gathers = [gather(h, gathered[h]) for h in range(parts)]
    scatters = [scatter(h, summed[h]) for h in range(parts)]
    advance(gathers[0], 1)
    tiles[slots] = jnp.zeros((width, width), tiles.dtype)
    for r in range(row_tiles):
        for c in range(column_tiles):
            found = jnp.int32(slots)
            for slot in range(slots):
                live = (tile_rows[0, slot] == r) & (tile_cols[0, slot] == c)
                found = jnp.where(live & (slot < tile_counts[0, 0]), slot, found)
            table[r * column_tiles + c] = found
    for h in range(parts):
        panel[h, pl.ds(pl.multiple_of(me * rows, 16), rows), :] = shard[:, lanes(h)]
    forwards = len(pieces) * (size // 2 - 1)
    for h in range(parts):
        advance(gathers[h], forwards if h == 0 else 0)
        if h + 1 < parts:
            advance(gathers[h + 1], 1)
        finish_steps(gathers[h])
        if h == 0:
            load.wait()
        if h + 1 < parts:
            weave(work(h, paired[h]), gathers[h + 1], 3, 2)
        else:
            weave(work(h, paired[h]), scatters[h - 1] if h else iter(()), 3, 1)
        advance(scatters[h], 1)
    for h in range(parts):
        finish_steps(scatters[h])
    for copies in gathered + paired + summed:
        drain(copies)


def front(shard, tiles, tile_rows, tile_cols, tile_counts, size):
    rows, comps = shard.shape
    slots, width, _ = tiles.shape
    parts = 2 if comps % (2 * LANES) == 0 else 1
    part = comps // parts
    row_span, column_span = rows * size, TC * width
    half = column_span // 2
    pieces = hypercube(size, rows, 16)
    narrow = jnp.bfloat16
    vmem, smem = pl.BlockSpec(memory_space=VMEM), pl.BlockSpec(memory_space=pltpu.SMEM)
    return pl.pallas_call(
        functools.partial(front_kernel, size, pieces),
        out_shape=(
            jax.ShapeDtypeStruct((rows, comps), narrow),
            jax.ShapeDtypeStruct((half, comps), narrow),
        ),
        in_specs=[vmem, pl.BlockSpec(memory_space=pltpu.HBM), smem, smem, smem],
        out_specs=[vmem, vmem],
        scratch_shapes=[
            VMEM((slots + 1, width, width), narrow),
            pltpu.SMEM((row_span // width * TC,), jnp.int32),
            VMEM((parts, row_span, part), narrow),
            VMEM((column_span, part), jnp.float32),
            VMEM((parts, half, part), narrow),
            VMEM((parts, half, part), narrow),
            VMEM((parts, column_span, part), narrow),
            VMEM((parts, row_span, part), narrow),
            VMEM((parts, size, rows, part), narrow),
            VMEM((parts, size, rows, part), narrow),
            pltpu.SemaphoreType.DMA,
            semaphores(2, parts, len(pieces), size),
            semaphores(2, parts, 2, TC),
            semaphores(2, parts, len(pieces), size),
        ],
        cost_estimate=pl.CostEstimate(flops=0, bytes_accessed=50_000_000, transcendentals=0),
        compiler_params=pltpu.CompilerParams(
            collective_id=5, has_side_effects=True, vmem_limit_bytes=52 << 20
        ),
    )(shard, tiles, tile_rows, tile_cols, tile_counts)


def lower(blocks):
    return [(i, j) for i in range(blocks) for j in range(i + 1)]


def gram_kernel(size, pieces, text, tag, out, both, other, own, gathered, land, outgoing, pair, sems):
    core = lax.axis_index("text")
    me = lax.axis_index("tag")
    rows = own.shape[1]
    pairs = lower(out.shape[0] // LANES)
    sibling = {"text": 1 - core}
    greet(tag_partners(size) + [sibling])
    for kind, panel in ((0, text), (1, tag)):
        gram = local_gram(panel[...])
        for at, (i, j) in enumerate(pairs):
            both[kind, at] = gram[i * LANES : (i + 1) * LANES, j * LANES : (j + 1) * LANES]
    swap = pltpu.make_async_remote_copy(
        src_ref=both.at[1 - core],
        dst_ref=other,
        send_sem=pair.at[0],
        recv_sem=pair.at[1],
        device_id=sibling,
        device_id_type=MESH,
    )
    swap.start()
    swap.wait()
    other[...] += both[core]

    def place(owner, lo, hi):
        return gathered.at[lo:hi, pl.ds(pl.multiple_of(owner * rows, 8), rows), :]

    def source(owner, lo, hi):
        return other.at[lo:hi, pl.ds(pl.multiple_of(owner * rows, 8), rows), :]

    def finish(lo, hi, total):
        own[lo:hi] = total

    copies = collect_start(pieces, source, land, sems.at[0], sems.at[1])
    collect(pieces, copies, source, land, outgoing, finish, sems.at[0], sems.at[1])
    more = spread(pieces, lambda lo, hi: own.at[lo:hi], place, sems.at[2], sems.at[3])
    gathered[:, pl.ds(pl.multiple_of(me * rows, 8), rows), :] = own[...]
    drain(copies)
    drain(more)
    for at, (i, j) in enumerate(pairs):
        block = gathered[at]
        if i == j:
            out[i * LANES : (i + 1) * LANES, j * LANES : (j + 1) * LANES] = block
        else:
            out[j * LANES : (j + 1) * LANES, i * LANES : (i + 1) * LANES] = block.T
            out[i * LANES : (i + 1) * LANES, j * LANES : (j + 1) * LANES] = block


def gram_sum(text, tag, size):
    comps = text.shape[1]
    rows = LANES // size
    count = len(lower(comps // LANES))
    pieces = hypercube(size, count, 1)
    square = jax.ShapeDtypeStruct((comps, comps), jnp.float32)
    return remote_call(
        functools.partial(gram_kernel, size, pieces),
        3,
        square,
        [
            VMEM((2, count, LANES, LANES), jnp.float32),
            VMEM((count, LANES, LANES), jnp.float32),
            VMEM((count, rows, LANES), jnp.float32),
            VMEM((count, LANES, LANES), jnp.float32),
            VMEM((size, count, rows, LANES), jnp.float32),
            VMEM((size, count, rows, LANES), jnp.float32),
            semaphores(2),
            semaphores(4, len(pieces), size),
        ],
        2,
    )(text, tag)


def swap_kernel(inverse, out, sems):
    core = lax.axis_index("text")
    sibling = {"text": 1 - core}
    greet([sibling])
    swap = pltpu.make_async_remote_copy(
        src_ref=inverse,
        dst_ref=out.at[core],
        send_sem=sems.at[0],
        recv_sem=sems.at[1],
        device_id=sibling,
        device_id_type=MESH,
    )
    swap.start()
    out[core] = inverse[...]
    swap.wait()


def swap_inverses(inverse):
    return remote_call(
        swap_kernel,
        4,
        jax.ShapeDtypeStruct((2,) + inverse.shape, jnp.float32),
        [semaphores(2)],
        1,
    )(inverse)


def shards(tile_values, tile_rows, tile_cols, tile_counts, panel_init):
    tiles = tile_values[0]
    rows = tile_rows[0]
    cols = tile_cols[0]
    count = tile_counts[0]
    width = tiles.shape[1]
    comps = panel_init.shape[1]
    text_size = lax.axis_size("text")
    tag_size = lax.axis_size("tag")
    column_span = TC * width
    share = column_span // text_size
    paired = text_size == 2 and LANES // tag_size >= 8
    if paired:
        text_mine, tag_mine = front(
            panel_init, tiles, tile_rows, tile_cols, tile_counts, tag_size
        )
    else:
        row_block = gather(panel_init, tag_size)
        row_span = row_block.shape[0]
        tag_partial = tile_product(
            tag_kernel, tiles, rows, cols, count, row_block, column_span, jnp.float32, []
        )
        column_block = lax.psum(tag_partial, "text").astype(jnp.bfloat16)
        tag_mine = lax.dynamic_slice_in_dim(
            column_block, lax.axis_index("text") * share, share, 0
        )
        text_partial = tile_product(
            text_kernel,
            tiles,
            rows,
            cols,
            count,
            column_block,
            row_span,
            jnp.bfloat16,
            [VMEM((row_span, comps), jnp.float32)],
        )
        text_mine = scatter_sum(text_partial, tag_size)
    if paired:
        gram = gram_sum(text_mine, tag_mine, tag_size)
        inverses = swap_inverses(inverse_factor(gram))
    else:
        text_gram, tag_gram = lax.psum(
            (local_gram(text_mine), local_gram(tag_mine)), ("text", "tag")
        )
        inverses = jnp.stack([inverse_factor(text_gram), inverse_factor(tag_gram)])
    text_total = text_mine.shape[0] * tag_size * text_size
    tag_total = column_span * tag_size
    return whiten(text_mine, tag_mine, inverses, math.sqrt(text_total), math.sqrt(tag_total))


def solution(mesh):
    in_specs = (
        P("text", "tag", None, None),
        P("text", "tag"),
        P("text", "tag"),
        P("text", "tag"),
        P(("text", "tag"), None),
    )
    out_specs = (P(("text", "tag"), None), P(("tag", "text"), None))
    return jax.shard_map(shards, mesh=mesh, in_specs=in_specs, out_specs=out_specs, check_vma=False)
```

```python
import functools
import math

import jax
import jax.numpy as jnp
from jax import lax
from jax.experimental import pallas as pl
from jax.experimental.pallas import tpu as pltpu
from jax.sharding import PartitionSpec as P

TC = 3
LANES = 128
VMEM = pltpu.VMEM


def tag_kernel(rows, cols, count, tile, panel, out):
    slot = pl.program_id(0)
    width = tile.shape[1]

    @pl.when(slot == 0)
    def _():
        out[...] = jnp.zeros_like(out)

    @pl.when(slot < count[0])
    def _():
        source = panel[pl.ds(pl.multiple_of(rows[slot] * width, width), width), :]
        into = pl.ds(pl.multiple_of(cols[slot] * width, width), width)
        out[into, :] += lax.dot_general(
            tile[0], source, (((0,), (0,)), ((), ())), preferred_element_type=jnp.float32
        )


def text_kernel(rows, cols, count, tile, panel, out, total):
    slot = pl.program_id(0)
    width = tile.shape[1]

    @pl.when(slot == 0)
    def _():
        total[...] = jnp.zeros_like(total)

    @pl.when(slot < count[0])
    def _():
        source = panel[pl.ds(pl.multiple_of(cols[slot] * width, width), width), :]
        into = pl.ds(pl.multiple_of(rows[slot] * width, width), width)
        total[into, :] += jnp.dot(tile[0], source, preferred_element_type=jnp.float32)

    @pl.when(slot == pl.num_programs(0) - 1)
    def _():
        out[...] = total[...].astype(out.dtype)


def tile_product(kernel, tiles, rows, cols, count, panel, out_rows, out_type, scratch):
    slots, width, _ = tiles.shape
    comps = panel.shape[1]

    def tile_at(slot, rows, cols, count):
        return (jnp.minimum(slot, count[0] - 1), 0, 0)

    def whole(slot, rows, cols, count):
        return (0, 0)

    return pl.pallas_call(
        kernel,
        out_shape=jax.ShapeDtypeStruct((out_rows, comps), out_type),
        grid_spec=pltpu.PrefetchScalarGridSpec(
            num_scalar_prefetch=3,
            grid=(slots,),
            in_specs=[
                pl.BlockSpec((1, width, width), tile_at),
                pl.BlockSpec(panel.shape, whole),
            ],
            out_specs=pl.BlockSpec((out_rows, comps), whole),
            scratch_shapes=scratch,
        ),
        compiler_params=pltpu.CompilerParams(vmem_limit_bytes=20 << 20),
    )(rows, cols, count, tiles, panel)


def eliminate(block):
    size = block.shape[0]
    groups = size // 8
    lane = lax.broadcasted_iota(jnp.int32, (8, size), 1)
    sub = lax.broadcasted_iota(jnp.int32, (8, size), 0)
    fixed = [jnp.full((8, size), s, jnp.int32) for s in range(8)]
    m = [block[8 * g : 8 * g + 8, :] for g in range(groups)]
    pivots = []

    def across(rows, k):
        return jnp.broadcast_to(rows[:, k : k + 1], (8, size))

    def down(rows, s):
        return jnp.broadcast_to(rows[s : s + 1, :], (8, size))

    def splat(rows, s):
        return jnp.take_along_axis(rows, fixed[s], axis=0, mode="promise_in_bounds")

    for g in range(groups):
        at = 8 * g
        inside = (lane >= at) & (lane < at + 8)
        own = [across(m[g], at + t) for t in range(8)]
        entry = {(s, t): splat(own[t], s) for t in range(8) for s in range(t, 8)}
        start = jnp.where(inside, jnp.where(lane == sub + at, 1.0, 0.0), m[g])
        rows = [down(start, s) for s in range(8)]
        pivot, steps = [None] * 8, []
        for t in range(0, 8, 2):
            a, b, c = entry[t, t], entry[t + 1, t], entry[t + 1, t + 1]
            det = a * c - b * b
            inverse, first = 1.0 / det, 1.0 / a
            later = range(t + 2, 8)
            left = {q: c * entry[q, t] - b * entry[q, t + 1] for q in later}
            right = {q: a * entry[q, t + 1] - b * entry[q, t] for q in later}
            for q in later:
                for s in range(q, 8):
                    taken = left[q] * entry[s, t] + right[q] * entry[s, t + 1]
                    entry[s, q] = entry[s, q] - inverse * taken
            left = {q: inverse * left[q] for q in later}
            right = {q: inverse * right[q] for q in later}
            upper, under = rows[t], rows[t + 1]
            for q in later:
                rows[q] = rows[q] - (left[q] * upper + right[q] * under)
            steps.append(
                (left, right, inverse * (c * upper - b * under), inverse * (a * under - b * upper))
            )
            rows[t + 1] = under - (b * first) * upper
            pivot[t], pivot[t + 1] = a, det * first
        for i in range(g + 1, groups):
            columns = [across(m[i], at + t) for t in range(8)]
            total = jnp.where(inside, 0.0, m[i])
            for t in range(0, 8, 2):
                left, right, upper, under = steps[t // 2]
                for q in range(t + 2, 8):
                    taken = left[q] * columns[t] + right[q] * columns[t + 1]
                    columns[q] = columns[q] - taken
                total = total - (columns[t] * upper + columns[t + 1] * under)
            m[i] = total
        done, kept = rows[0], pivot[0]
        for t in range(1, 8):
            done = jnp.where(sub == t, rows[t], done)
            kept = jnp.where(sub == t, pivot[t], kept)
        m[g] = done
        pivots.append(kept)
    out = []
    for g in range(groups):
        kept = jnp.where(lane <= sub + 8 * g, m[g], 0.0)
        out.append(kept * lax.rsqrt(pivots[g]))
    return jnp.concatenate(out, axis=0)


def factor_in_place(work, scale, out):
    size = work.shape[0]
    blocks = size // LANES
    exact = lax.Precision.HIGHEST
    lane = lax.broadcasted_iota(jnp.int32, (LANES, LANES), 1)
    sub = lax.broadcasted_iota(jnp.int32, (LANES, LANES), 0)
    tall = []
    for b in range(blocks):
        lo, hi = b * LANES, (b + 1) * LANES
        diagonal = jnp.where(lane == sub, work[lo:hi, lo:hi], 0.0)
        scale[:, lo:hi] = lax.rsqrt(jnp.sum(diagonal, axis=0, keepdims=True))
        tall.append(lax.rsqrt(jnp.sum(diagonal, axis=1, keepdims=True)))
    for b in range(blocks):
        lo, hi = b * LANES, (b + 1) * LANES
        work[lo:hi, :] = (work[lo:hi, :] * tall[b]) * scale[...]

    for b in range(blocks):
        lo, hi = b * LANES, (b + 1) * LANES
        inverse = eliminate(work[lo:hi, lo:hi])
        row = jnp.dot(
            inverse, work[lo:hi, :], preferred_element_type=jnp.float32, precision=exact
        )
        work[lo:hi, :] = row
        work[lo:hi, lo:hi] = inverse
        if hi < size:
            work[hi:, lo:hi] = jnp.zeros((size - hi, LANES), jnp.float32)
            work[hi:, :] -= lax.dot_general(
                work[lo:hi, hi:],
                work[lo:hi, :],
                (((0,), (0,)), ((), ())),
                preferred_element_type=jnp.float32,
                precision=exact,
            )
        lanes = lax.broadcasted_iota(jnp.int32, (LANES, size), 1)
        subs = lax.broadcasted_iota(jnp.int32, (LANES, size), 0) + lo
        out[lo:hi, :] = jnp.where(lanes <= subs, work[lo:hi, :] * scale[...], 0.0)


def factor_kernel(gram, out, work, scale):
    work[...] = gram[...]
    factor_in_place(work, scale, out)


def inverse_factor(gram):
    return pl.pallas_call(
        factor_kernel,
        out_shape=jax.ShapeDtypeStruct(gram.shape, jnp.float32),
        in_specs=[pl.BlockSpec(memory_space=VMEM)],
        out_specs=pl.BlockSpec(memory_space=VMEM),
        scratch_shapes=[VMEM(gram.shape, jnp.float32), VMEM((1, gram.shape[1]), jnp.float32)],
        compiler_params=pltpu.CompilerParams(vmem_limit_bytes=16 << 20),
    )(gram)


def white_kernel(text_scale, tag_scale, text, tag, inverses, text_out, tag_out):
    for panel, kind, out, scale in ((text, 0, text_out, text_scale), (tag, 1, tag_out, tag_scale)):
        whole = inverses[kind] * scale
        high = whole.astype(jnp.bfloat16)
        low = (whole - high.astype(jnp.float32)).astype(jnp.bfloat16)
        rows = panel.shape[0]
        step = min(rows, LANES)
        for at in range(0, rows, step):
            part = panel[at : at + step, :]
            dims = (((1,), (1,)), ((), ()))
            out[at : at + step, :] = lax.dot_general(
                part, high, dims, preferred_element_type=jnp.float32
            ) + lax.dot_general(part, low, dims, preferred_element_type=jnp.float32)


def whiten(text, tag, inverses, text_scale, tag_scale):
    return pl.pallas_call(
        functools.partial(white_kernel, text_scale, tag_scale),
        out_shape=(
            jax.ShapeDtypeStruct(text.shape, jnp.float32),
            jax.ShapeDtypeStruct(tag.shape, jnp.float32),
        ),
        in_specs=[pl.BlockSpec(memory_space=VMEM)] * 3,
        out_specs=[pl.BlockSpec(memory_space=VMEM)] * 2,
        compiler_params=pltpu.CompilerParams(vmem_limit_bytes=16 << 20),
    )(text, tag, inverses)


def local_gram(panel):
    return lax.dot_general(
        panel, panel, (((0,), (0,)), ((), ())), preferred_element_type=jnp.float32
    )


MESH = pl.DeviceIdType.MESH


def flip(me, offset):
    total, bit = me, 1
    while bit <= offset:
        if offset & bit:
            total = total + bit * (1 - 2 * lax.rem(lax.div(me, bit), 2))
        bit *= 2
    return total


def hypercube(size, rows, unit):
    bits = size.bit_length() - 1
    down = tuple(reversed(range(bits)))
    orders = [down]
    if bits >= 3:
        orders += [down[:-2] + (down[-1], down[-2]), (0, 1) + down[:-2]]
    units = rows // unit
    pieces, at = [], 0
    for number, order in enumerate(orders):
        here = units // len(orders) + (1 if number < units % len(orders) else 0)
        if here:
            pieces.append((order, at * unit, (at + here) * unit))
            at += here
    return pieces


def arrivals(order, stage):
    found = [1 << order[stage]]
    for bit in order[:stage]:
        found += [offset | 1 << bit for offset in found]
    return found


def greet(groups):
    barrier = pltpu.get_barrier_semaphore()
    for device in groups:
        pl.semaphore_signal(barrier, inc=1, device_id=device, device_id_type=MESH)
    pl.semaphore_wait(barrier, len(groups))


def tag_partners(size):
    me = lax.axis_index("tag")
    return [{"tag": flip(me, 1 << bit)} for bit in range(size.bit_length() - 1)]


def spread(pieces, source, place, send, recv):
    me = lax.axis_index("tag")
    copies = {}

    def go(number, offset, bit):
        order, lo, hi = pieces[number]
        owner = flip(me, offset)
        to = offset | 1 << bit
        copies[number, to] = pltpu.make_async_remote_copy(
            src_ref=source(lo, hi) if offset == 0 else place(owner, lo, hi),
            dst_ref=place(owner, lo, hi),
            send_sem=send.at[number, to],
            recv_sem=recv.at[number, to],
            device_id={"tag": flip(me, 1 << bit)},
            device_id_type=MESH,
        )
        copies[number, to].start()

    bits = len(pieces[0][0])
    for stage in range(bits):
        for number, (order, _, _) in enumerate(pieces):
            go(number, 0, order[stage])
    for stage in range(bits):
        for turn in range(1 << stage):
            for number, (order, _, _) in enumerate(pieces):
                offset = arrivals(order, stage)[turn]
                copies[number, offset].wait_recv()
                for later in range(stage + 1, bits):
                    go(number, offset, order[later])
    return copies


def collect_start(pieces, source, land, send, recv):
    me = lax.axis_index("tag")
    copies = {}
    last = len(pieces[0][0]) - 1
    for turn in range(1 << last):
        for number, (order, lo, hi) in enumerate(pieces):
            offset = arrivals(order, last)[turn]
            copies[number, offset] = pltpu.make_async_remote_copy(
                src_ref=source(flip(me, offset), lo, hi),
                dst_ref=land.at[offset, lo:hi],
                send_sem=send.at[number, offset],
                recv_sem=recv.at[number, offset],
                device_id={"tag": flip(me, 1 << order[last])},
                device_id_type=MESH,
            )
            copies[number, offset].start()
    return copies


def collect(pieces, copies, source, land, outgoing, finish, send, recv):
    me = lax.axis_index("tag")
    bits = len(pieces[0][0])

    def summed(number, offset, stage):
        order, lo, hi = pieces[number]
        total = source(flip(me, offset), lo, hi)[...].astype(jnp.float32)
        for later in reversed(range(stage + 1, bits)):
            come = offset | 1 << order[later]
            copies[number, come].wait_recv()
            total = total + land[come, lo:hi].astype(jnp.float32)
        return total

    for stage in reversed(range(bits - 1)):
        for turn in range(1 << stage):
            for number, (order, lo, hi) in enumerate(pieces):
                offset = arrivals(order, stage)[turn]
                outgoing[offset, lo:hi] = summed(number, offset, stage).astype(outgoing.dtype)
                copies[number, offset] = pltpu.make_async_remote_copy(
                    src_ref=outgoing.at[offset, lo:hi],
                    dst_ref=land.at[offset, lo:hi],
                    send_sem=send.at[number, offset],
                    recv_sem=recv.at[number, offset],
                    device_id={"tag": flip(me, 1 << order[stage])},
                    device_id_type=MESH,
                )
                copies[number, offset].start()
    for number, (_, lo, hi) in enumerate(pieces):
        finish(lo, hi, summed(number, 0, -1))


def drain(copies):
    for copy in copies.values():
        copy.wait_send()


def gather_kernel(size, pieces, shard, out, send, recv):
    rows = shard.shape[0]
    greet(tag_partners(size))

    def place(owner, lo, hi):
        return out.at[pl.ds(pl.multiple_of(owner * rows + lo, 16), hi - lo), :]

    copies = spread(pieces, lambda lo, hi: shard.at[lo:hi, :], place, send, recv)
    me = lax.axis_index("tag")
    out[pl.ds(pl.multiple_of(me * rows, 16), rows), :] = shard[...]
    drain(copies)


def remote_call(kernel, number, out_shape, scratch, count):
    many = isinstance(out_shape, tuple)
    spec = pl.BlockSpec(memory_space=VMEM)
    return pl.pallas_call(
        kernel,
        out_shape=out_shape,
        in_specs=[spec] * count,
        out_specs=[spec] * len(out_shape) if many else spec,
        scratch_shapes=scratch,
        cost_estimate=pl.CostEstimate(flops=0, bytes_accessed=50_000_000, transcendentals=0),
        compiler_params=pltpu.CompilerParams(
            collective_id=number, has_side_effects=True, vmem_limit_bytes=20 << 20
        ),
    )


def semaphores(*shape):
    return pltpu.SemaphoreType.DMA(shape)


def gather(shard, size):
    rows, comps = shard.shape
    pieces = hypercube(size, rows, 16)
    return remote_call(
        functools.partial(gather_kernel, size, pieces),
        0,
        jax.ShapeDtypeStruct((rows * size, comps), shard.dtype),
        [semaphores(len(pieces), size), semaphores(len(pieces), size)],
        1,
    )(shard)


def scatter_kernel(size, pieces, partial, out, land, outgoing, send, recv):
    rows = out.shape[0]
    greet(tag_partners(size))

    def source(owner, lo, hi):
        return partial.at[pl.ds(pl.multiple_of(owner * rows + lo, 16), hi - lo), :]

    def finish(lo, hi, total):
        out[lo:hi, :] = total.astype(out.dtype)

    copies = collect_start(pieces, source, land, send, recv)
    collect(pieces, copies, source, land, outgoing, finish, send, recv)
    drain(copies)


def scatter_sum(partial, size):
    rows, comps = partial.shape[0] // size, partial.shape[1]
    pieces = hypercube(size, rows, 16)
    return remote_call(
        functools.partial(scatter_kernel, size, pieces),
        2,
        jax.ShapeDtypeStruct((rows, comps), jnp.bfloat16),
        [
            VMEM((size, rows, comps), jnp.bfloat16),
            VMEM((size, rows, comps), jnp.bfloat16),
            semaphores(len(pieces), size),
            semaphores(len(pieces), size),
        ],
        1,
    )(partial)


def spread_steps(pieces, source, place, send, recv, copies):
    me = lax.axis_index("tag")

    def go(number, offset, bit):
        order, lo, hi = pieces[number]
        owner = flip(me, offset)
        to = offset | 1 << bit
        copies[number, to] = pltpu.make_async_remote_copy(
            src_ref=source(lo, hi) if offset == 0 else place(owner, lo, hi),
            dst_ref=place(owner, lo, hi),
            send_sem=send.at[number, to],
            recv_sem=recv.at[number, to],
            device_id={"tag": flip(me, 1 << bit)},
            device_id_type=MESH,
        )
        copies[number, to].start()

    bits = len(pieces[0][0])
    for stage in range(bits):
        for number, (order, _, _) in enumerate(pieces):
            go(number, 0, order[stage])
    yield
    for stage in range(bits):
        for turn in range(1 << stage):
            for number, (order, _, _) in enumerate(pieces):
                offset = arrivals(order, stage)[turn]
                copies[number, offset].wait_recv()
                for later in range(stage + 1, bits):
                    go(number, offset, order[later])
                yield number, offset


def collect_steps(pieces, source, land, outgoing, finish, send, recv, copies, before):
    me = lax.axis_index("tag")
    bits = len(pieces[0][0])

    def go(number, offset, bit, ref):
        _, lo, hi = pieces[number]
        copies[number, offset] = pltpu.make_async_remote_copy(
            src_ref=ref,
            dst_ref=land(offset, lo, hi),
            send_sem=send.at[number, offset],
            recv_sem=recv.at[number, offset],
            device_id={"tag": flip(me, 1 << bit)},
            device_id_type=MESH,
        )
        copies[number, offset].start()

    def summed(number, offset, stage):
        order, lo, hi = pieces[number]
        total = source(flip(me, offset), lo, hi)[...].astype(jnp.float32)
        for later in reversed(range(stage + 1, bits)):
            come = offset | 1 << order[later]
            copies[number, come].wait_recv()
            total = total + land(come, lo, hi)[...].astype(jnp.float32)
        return total

    last = bits - 1
    for turn in reversed(range(1 << last)):
        for number, (order, lo, hi) in enumerate(pieces):
            offset = arrivals(order, last)[turn]
            before(offset)
            go(number, offset, order[last], source(flip(me, offset), lo, hi))
    before(0)
    yield
    for stage in reversed(range(last)):
        for turn in reversed(range(1 << stage)):
            for number, (order, lo, hi) in enumerate(pieces):
                offset = arrivals(order, stage)[turn]
                leaving = outgoing(offset, lo, hi)
                leaving[...] = summed(number, offset, stage).astype(leaving.dtype)
                go(number, offset, order[stage], leaving)
                yield
    for number, (_, lo, hi) in enumerate(pieces):
        finish(lo, hi, summed(number, 0, -1))
        yield


def finish_steps(steps):
    for _ in steps:
        pass


def front_kernel(
    size, pieces, shard, stored, tile_rows, tile_cols, tile_counts, text_out, tag_out,
    tiles, table, panel, total, leaving, arrived, columns, partial, land, outgoing,
    tile_sem, gather_sems, pair_sems, scatter_sems,
):
    core = lax.axis_index("text")
    me = lax.axis_index("tag")
    sibling = {"text": 1 - core}
    slots, width, _ = stored.shape
    rows = shard.shape[0]
    row_span, column_span = panel.shape[0], columns.shape[0]
    row_tiles, column_tiles = row_span // width, column_span // width
    share = width // rows
    half = column_span // 2
    chunk = half // column_tiles
    load = pltpu.make_async_copy(stored, tiles.at[0:slots], tile_sem)
    load.start()
    greet(tag_partners(size) + [sibling])

    def place(owner, lo, hi):
        return panel.at[pl.ds(pl.multiple_of(owner * rows + lo, 16), hi - lo), :]

    def source(owner, lo, hi):
        return partial.at[pl.ds(pl.multiple_of(owner * rows + lo, 16), hi - lo), :]

    def row_tile(distance):
        return lax.div(flip(me, distance * share), share)

    def tile_rows_of(r):
        return pl.ds(pl.multiple_of(r * width, width), width)

    gathered, paired, summed = {}, {}, {}
    steps = spread_steps(
        pieces,
        lambda lo, hi: shard.at[lo:hi, :],
        place,
        gather_sems.at[0],
        gather_sems.at[1],
        gathered,
    )
    next(steps)
    tiles[slots] = jnp.zeros((width, width), tiles.dtype)
    for r in range(row_tiles):
        for c in range(column_tiles):
            found = jnp.int32(slots)
            for slot in range(slots):
                live = (tile_rows[0, slot] == r) & (tile_cols[0, slot] == c)
                found = jnp.where(live & (slot < tile_counts[0, 0]), slot, found)
            table[r * column_tiles + c] = found
    panel[pl.ds(pl.multiple_of(me * rows, 16), rows), :] = shard[...]

    def swap(phase, number, src, dst):
        copy = pltpu.make_async_remote_copy(
            src_ref=src,
            dst_ref=dst,
            send_sem=pair_sems.at[0, phase, number],
            recv_sem=pair_sems.at[1, phase, number],
            device_id=sibling,
            device_id_type=MESH,
        )
        copy.start()
        paired[phase, number] = copy

    finished = []

    def tag_products(distance):
        if not finished:
            load.wait()
        r = row_tile(distance)
        block = panel[tile_rows_of(r), :]
        sent = False
        for turn in range(column_tiles):
            c = core * turn + (1 - core) * (column_tiles - 1 - turn)
            product = lax.dot_general(
                tiles[table[r * column_tiles + c]],
                block,
                (((0,), (0,)), ((), ())),
                preferred_element_type=jnp.float32,
            )
            if not finished:
                total[tile_rows_of(c), :] = product
            else:
                total[tile_rows_of(c), :] += product
            if len(finished) == row_tiles - 1 and not sent and (turn + 1) * width >= half:
                sent = True
                for number in range(column_tiles):
                    lo = number * chunk
                    theirs = pl.ds(pl.multiple_of((1 - core) * half + lo, 16), chunk)
                    leaving[lo : lo + chunk, :] = total[theirs, :].astype(leaving.dtype)
                    swap(0, number, leaving.at[lo : lo + chunk, :], arrived.at[lo : lo + chunk, :])
        finished.append(distance)

    missing = {(number, offset) for number in range(len(pieces)) for offset in range(1, size)}
    for event in steps:
        missing.discard(event)
        waiting = {offset // share for _, offset in missing}
        for distance in range(row_tiles):
            if distance not in waiting and distance not in finished:
                tag_products(distance)

    for number in range(column_tiles):
        lo = number * chunk
        ours = pl.ds(pl.multiple_of(core * half + lo, 16), chunk)
        paired[0, number].wait_recv()
        value = total[ours, :] + arrived[lo : lo + chunk, :].astype(jnp.float32)
        value = value.astype(columns.dtype)
        columns[ours, :] = value
        tag_out[lo : lo + chunk, :] = value
        swap(1, number, columns.at[ours, :], columns.at[ours, :])
    for number in range(column_tiles):
        paired[1, number].wait_recv()

    ready = set()

    def text_products(offset):
        for distance in [offset // share] if offset else range(row_tiles):
            if distance in ready:
                continue
            ready.add(distance)
            r = row_tile(distance)
            value = None
            for c in range(column_tiles):
                product = jnp.dot(
                    tiles[table[r * column_tiles + c]],
                    columns[c * width : (c + 1) * width, :],
                    preferred_element_type=jnp.float32,
                )
                value = product if value is None else value + product
            partial[tile_rows_of(r), :] = value.astype(partial.dtype)

    def done(lo, hi, value):
        text_out[lo:hi, :] = value.astype(text_out.dtype)

    finish_steps(
        collect_steps(
            pieces,
            source,
            lambda offset, lo, hi: land.at[offset, lo:hi, :],
            lambda offset, lo, hi: outgoing.at[offset, lo:hi, :],
            done,
            scatter_sems.at[0],
            scatter_sems.at[1],
            summed,
            text_products,
        )
    )
    for copies in (gathered, paired, summed):
        drain(copies)


def front(shard, tiles, tile_rows, tile_cols, tile_counts, size):
    rows, comps = shard.shape
    slots, width, _ = tiles.shape
    row_span, column_span = rows * size, TC * width
    half = column_span // 2
    pieces = hypercube(size, rows, 16)
    narrow = jnp.bfloat16
    vmem, smem = pl.BlockSpec(memory_space=VMEM), pl.BlockSpec(memory_space=pltpu.SMEM)
    return pl.pallas_call(
        functools.partial(front_kernel, size, pieces),
        out_shape=(
            jax.ShapeDtypeStruct((rows, comps), narrow),
            jax.ShapeDtypeStruct((half, comps), narrow),
        ),
        in_specs=[vmem, pl.BlockSpec(memory_space=pltpu.HBM), smem, smem, smem],
        out_specs=[vmem, vmem],
        scratch_shapes=[
            VMEM((slots + 1, width, width), narrow),
            pltpu.SMEM((row_span // width * TC,), jnp.int32),
            VMEM((row_span, comps), narrow),
            VMEM((column_span, comps), jnp.float32),
            VMEM((half, comps), narrow),
            VMEM((half, comps), narrow),
            VMEM((column_span, comps), narrow),
            VMEM((row_span, comps), narrow),
            VMEM((size, rows, comps), narrow),
            VMEM((size, rows, comps), narrow),
            pltpu.SemaphoreType.DMA,
            semaphores(2, len(pieces), size),
            semaphores(2, 2, TC),
            semaphores(2, len(pieces), size),
        ],
        cost_estimate=pl.CostEstimate(flops=0, bytes_accessed=50_000_000, transcendentals=0),
        compiler_params=pltpu.CompilerParams(
            collective_id=5, has_side_effects=True, vmem_limit_bytes=52 << 20
        ),
    )(shard, tiles, tile_rows, tile_cols, tile_counts)


def lower(blocks):
    return [(i, j) for i in range(blocks) for j in range(i + 1)]


def gram_kernel(size, pieces, text, tag, out, both, other, own, gathered, land, outgoing, pair, sems):
    core = lax.axis_index("text")
    me = lax.axis_index("tag")
    rows = own.shape[1]
    pairs = lower(out.shape[0] // LANES)
    sibling = {"text": 1 - core}
    greet(tag_partners(size) + [sibling])
    for kind, panel in ((0, text), (1, tag)):
        gram = local_gram(panel[...])
        for at, (i, j) in enumerate(pairs):
            both[kind, at] = gram[i * LANES : (i + 1) * LANES, j * LANES : (j + 1) * LANES]
    swap = pltpu.make_async_remote_copy(
        src_ref=both.at[1 - core],
        dst_ref=other,
        send_sem=pair.at[0],
        recv_sem=pair.at[1],
        device_id=sibling,
        device_id_type=MESH,
    )
    swap.start()
    swap.wait()
    other[...] += both[core]

    def place(owner, lo, hi):
        return gathered.at[lo:hi, pl.ds(pl.multiple_of(owner * rows, 8), rows), :]

    def source(owner, lo, hi):
        return other.at[lo:hi, pl.ds(pl.multiple_of(owner * rows, 8), rows), :]

    def finish(lo, hi, total):
        own[lo:hi] = total

    copies = {}
    finish_steps(
        collect_steps(
            pieces,
            source,
            lambda offset, lo, hi: land.at[offset, lo:hi],
            lambda offset, lo, hi: outgoing.at[offset, lo:hi],
            finish,
            sems.at[0],
            sems.at[1],
            copies,
            lambda offset: None,
        )
    )
    more = spread(pieces, lambda lo, hi: own.at[lo:hi], place, sems.at[2], sems.at[3])
    gathered[:, pl.ds(pl.multiple_of(me * rows, 8), rows), :] = own[...]
    drain(copies)
    drain(more)
    for at, (i, j) in enumerate(pairs):
        block = gathered[at]
        if i == j:
            out[i * LANES : (i + 1) * LANES, j * LANES : (j + 1) * LANES] = block
        else:
            out[j * LANES : (j + 1) * LANES, i * LANES : (i + 1) * LANES] = block.T
            out[i * LANES : (i + 1) * LANES, j * LANES : (j + 1) * LANES] = block


def gram_sum(text, tag, size):
    comps = text.shape[1]
    rows = LANES // size
    count = len(lower(comps // LANES))
    pieces = hypercube(size, count, 1)
    square = jax.ShapeDtypeStruct((comps, comps), jnp.float32)
    return remote_call(
        functools.partial(gram_kernel, size, pieces),
        3,
        square,
        [
            VMEM((2, count, LANES, LANES), jnp.float32),
            VMEM((count, LANES, LANES), jnp.float32),
            VMEM((count, rows, LANES), jnp.float32),
            VMEM((count, LANES, LANES), jnp.float32),
            VMEM((size, count, rows, LANES), jnp.float32),
            VMEM((size, count, rows, LANES), jnp.float32),
            semaphores(2),
            semaphores(4, len(pieces), size),
        ],
        2,
    )(text, tag)


def swap_kernel(inverse, out, sems):
    core = lax.axis_index("text")
    sibling = {"text": 1 - core}
    greet([sibling])
    swap = pltpu.make_async_remote_copy(
        src_ref=inverse,
        dst_ref=out.at[core],
        send_sem=sems.at[0],
        recv_sem=sems.at[1],
        device_id=sibling,
        device_id_type=MESH,
    )
    swap.start()
    out[core] = inverse[...]
    swap.wait()


def swap_inverses(inverse):
    return remote_call(
        swap_kernel,
        4,
        jax.ShapeDtypeStruct((2,) + inverse.shape, jnp.float32),
        [semaphores(2)],
        1,
    )(inverse)


def shards(tile_values, tile_rows, tile_cols, tile_counts, panel_init):
    tiles = tile_values[0]
    rows = tile_rows[0]
    cols = tile_cols[0]
    count = tile_counts[0]
    width = tiles.shape[1]
    comps = panel_init.shape[1]
    text_size = lax.axis_size("text")
    tag_size = lax.axis_size("tag")
    column_span = TC * width
    share = column_span // text_size
    paired = text_size == 2 and LANES // tag_size >= 8
    if paired:
        text_mine, tag_mine = front(
            panel_init, tiles, tile_rows, tile_cols, tile_counts, tag_size
        )
    else:
        row_block = gather(panel_init, tag_size)
        row_span = row_block.shape[0]
        tag_partial = tile_product(
            tag_kernel, tiles, rows, cols, count, row_block, column_span, jnp.float32, []
        )
        column_block = lax.psum(tag_partial, "text").astype(jnp.bfloat16)
        tag_mine = lax.dynamic_slice_in_dim(
            column_block, lax.axis_index("text") * share, share, 0
        )
        text_partial = tile_product(
            text_kernel,
            tiles,
            rows,
            cols,
            count,
            column_block,
            row_span,
            jnp.bfloat16,
            [VMEM((row_span, comps), jnp.float32)],
        )
        text_mine = scatter_sum(text_partial, tag_size)
    if paired:
        gram = gram_sum(text_mine, tag_mine, tag_size)
        inverses = swap_inverses(inverse_factor(gram))
    else:
        text_gram, tag_gram = lax.psum(
            (local_gram(text_mine), local_gram(tag_mine)), ("text", "tag")
        )
        inverses = jnp.stack([inverse_factor(text_gram), inverse_factor(tag_gram)])
    text_total = text_mine.shape[0] * tag_size * text_size
    tag_total = column_span * tag_size
    return whiten(text_mine, tag_mine, inverses, math.sqrt(text_total), math.sqrt(tag_total))


def solution(mesh):
    in_specs = (
        P("text", "tag", None, None),
        P("text", "tag"),
        P("text", "tag"),
        P("text", "tag"),
        P(("text", "tag"), None),
    )
    out_specs = (P(("text", "tag"), None), P(("tag", "text"), None))
    return jax.shard_map(shards, mesh=mesh, in_specs=in_specs, out_specs=out_specs, check_vma=False)
```

```python
import functools
import math

import jax
import jax.numpy as jnp
from jax import lax
from jax.experimental import pallas as pl
from jax.experimental.pallas import tpu as pltpu
from jax.sharding import PartitionSpec as P

TC = 3
LANES = 128
VMEM = pltpu.VMEM


def tag_kernel(rows, cols, count, tile, panel, out):
    slot = pl.program_id(0)
    width = tile.shape[1]

    @pl.when(slot == 0)
    def _():
        out[...] = jnp.zeros_like(out)

    @pl.when(slot < count[0])
    def _():
        source = panel[pl.ds(pl.multiple_of(rows[slot] * width, width), width), :]
        into = pl.ds(pl.multiple_of(cols[slot] * width, width), width)
        out[into, :] += lax.dot_general(
            tile[0], source, (((0,), (0,)), ((), ())), preferred_element_type=jnp.float32
        )


def text_kernel(rows, cols, count, tile, panel, out, total):
    slot = pl.program_id(0)
    width = tile.shape[1]

    @pl.when(slot == 0)
    def _():
        total[...] = jnp.zeros_like(total)

    @pl.when(slot < count[0])
    def _():
        source = panel[pl.ds(pl.multiple_of(cols[slot] * width, width), width), :]
        into = pl.ds(pl.multiple_of(rows[slot] * width, width), width)
        total[into, :] += jnp.dot(tile[0], source, preferred_element_type=jnp.float32)

    @pl.when(slot == pl.num_programs(0) - 1)
    def _():
        out[...] = total[...].astype(out.dtype)


def tile_product(kernel, tiles, rows, cols, count, panel, out_rows, out_type, scratch):
    slots, width, _ = tiles.shape
    comps = panel.shape[1]

    def tile_at(slot, rows, cols, count):
        return (jnp.minimum(slot, count[0] - 1), 0, 0)

    def whole(slot, rows, cols, count):
        return (0, 0)

    return pl.pallas_call(
        kernel,
        out_shape=jax.ShapeDtypeStruct((out_rows, comps), out_type),
        grid_spec=pltpu.PrefetchScalarGridSpec(
            num_scalar_prefetch=3,
            grid=(slots,),
            in_specs=[
                pl.BlockSpec((1, width, width), tile_at),
                pl.BlockSpec(panel.shape, whole),
            ],
            out_specs=pl.BlockSpec((out_rows, comps), whole),
            scratch_shapes=scratch,
        ),
        compiler_params=pltpu.CompilerParams(vmem_limit_bytes=20 << 20),
    )(rows, cols, count, tiles, panel)


def eliminate(block):
    size = block.shape[0]
    groups = size // 8
    lane = lax.broadcasted_iota(jnp.int32, (8, size), 1)
    sub = lax.broadcasted_iota(jnp.int32, (8, size), 0)
    fixed = [jnp.full((8, size), s, jnp.int32) for s in range(8)]
    m = [block[8 * g : 8 * g + 8, :] for g in range(groups)]
    pivots = []

    def across(rows, k):
        return jnp.broadcast_to(rows[:, k : k + 1], (8, size))

    def down(rows, s):
        return jnp.broadcast_to(rows[s : s + 1, :], (8, size))

    def splat(rows, s):
        return jnp.take_along_axis(rows, fixed[s], axis=0, mode="promise_in_bounds")

    for g in range(groups):
        at = 8 * g
        inside = (lane >= at) & (lane < at + 8)
        own = [across(m[g], at + t) for t in range(8)]
        entry = {(s, t): splat(own[t], s) for t in range(8) for s in range(t, 8)}
        start = jnp.where(inside, jnp.where(lane == sub + at, 1.0, 0.0), m[g])
        rows = [down(start, s) for s in range(8)]
        pivot, steps = [None] * 8, []
        for t in range(0, 8, 2):
            a, b, c = entry[t, t], entry[t + 1, t], entry[t + 1, t + 1]
            det = a * c - b * b
            inverse, first = 1.0 / det, 1.0 / a
            later = range(t + 2, 8)
            left = {q: c * entry[q, t] - b * entry[q, t + 1] for q in later}
            right = {q: a * entry[q, t + 1] - b * entry[q, t] for q in later}
            for q in later:
                for s in range(q, 8):
                    taken = left[q] * entry[s, t] + right[q] * entry[s, t + 1]
                    entry[s, q] = entry[s, q] - inverse * taken
            left = {q: inverse * left[q] for q in later}
            right = {q: inverse * right[q] for q in later}
            upper, under = rows[t], rows[t + 1]
            for q in later:
                rows[q] = rows[q] - (left[q] * upper + right[q] * under)
            steps.append(
                (left, right, inverse * (c * upper - b * under), inverse * (a * under - b * upper))
            )
            rows[t + 1] = under - (b * first) * upper
            pivot[t], pivot[t + 1] = a, det * first
        for i in range(g + 1, groups):
            columns = [across(m[i], at + t) for t in range(8)]
            total = jnp.where(inside, 0.0, m[i])
            for t in range(0, 8, 2):
                left, right, upper, under = steps[t // 2]
                for q in range(t + 2, 8):
                    taken = left[q] * columns[t] + right[q] * columns[t + 1]
                    columns[q] = columns[q] - taken
                total = total - (columns[t] * upper + columns[t + 1] * under)
            m[i] = total
        done, kept = rows[0], pivot[0]
        for t in range(1, 8):
            done = jnp.where(sub == t, rows[t], done)
            kept = jnp.where(sub == t, pivot[t], kept)
        m[g] = done
        pivots.append(kept)
    out = []
    for g in range(groups):
        kept = jnp.where(lane <= sub + 8 * g, m[g], 0.0)
        out.append(kept * lax.rsqrt(pivots[g]))
    return jnp.concatenate(out, axis=0)


def factor_in_place(work, scale, store):
    size = work.shape[0]
    blocks = size // LANES
    exact = lax.Precision.HIGHEST
    lane = lax.broadcasted_iota(jnp.int32, (LANES, LANES), 1)
    sub = lax.broadcasted_iota(jnp.int32, (LANES, LANES), 0)
    tall = []
    for b in range(blocks):
        lo, hi = b * LANES, (b + 1) * LANES
        diagonal = jnp.where(lane == sub, work[lo:hi, lo:hi], 0.0)
        scale[:, lo:hi] = lax.rsqrt(jnp.sum(diagonal, axis=0, keepdims=True))
        tall.append(lax.rsqrt(jnp.sum(diagonal, axis=1, keepdims=True)))
    for b in range(blocks):
        lo, hi = b * LANES, (b + 1) * LANES
        work[lo:hi, :] = (work[lo:hi, :] * tall[b]) * scale[...]

    for b in range(blocks):
        lo, hi = b * LANES, (b + 1) * LANES
        inverse = eliminate(work[lo:hi, lo:hi])
        row = jnp.dot(
            inverse, work[lo:hi, :], preferred_element_type=jnp.float32, precision=exact
        )
        work[lo:hi, :] = row
        work[lo:hi, lo:hi] = inverse
        if hi < size:
            work[hi:, lo:hi] = jnp.zeros((size - hi, LANES), jnp.float32)
            work[hi:, :] -= lax.dot_general(
                work[lo:hi, hi:],
                work[lo:hi, :],
                (((0,), (0,)), ((), ())),
                preferred_element_type=jnp.float32,
                precision=exact,
            )
        lanes = lax.broadcasted_iota(jnp.int32, (LANES, size), 1)
        subs = lax.broadcasted_iota(jnp.int32, (LANES, size), 0) + lo
        store(lo, hi, jnp.where(lanes <= subs, work[lo:hi, :] * scale[...], 0.0))


def factor_kernel(gram, out, work, scale):
    def store(lo, hi, value):
        out[lo:hi, :] = value

    work[...] = gram[...]
    factor_in_place(work, scale, store)


def inverse_factor(gram):
    return pl.pallas_call(
        factor_kernel,
        out_shape=jax.ShapeDtypeStruct(gram.shape, jnp.float32),
        in_specs=[pl.BlockSpec(memory_space=VMEM)],
        out_specs=pl.BlockSpec(memory_space=VMEM),
        scratch_shapes=[VMEM(gram.shape, jnp.float32), VMEM((1, gram.shape[1]), jnp.float32)],
        compiler_params=pltpu.CompilerParams(vmem_limit_bytes=16 << 20),
    )(gram)


def white_kernel(text_scale, tag_scale, text, tag, inverses, text_out, tag_out):
    for panel, kind, out, scale in ((text, 0, text_out, text_scale), (tag, 1, tag_out, tag_scale)):
        whole = inverses[kind] * scale
        high = whole.astype(jnp.bfloat16)
        low = (whole - high.astype(jnp.float32)).astype(jnp.bfloat16)
        rows = panel.shape[0]
        step = min(rows, LANES)
        for at in range(0, rows, step):
            part = panel[at : at + step, :]
            dims = (((1,), (1,)), ((), ()))
            out[at : at + step, :] = lax.dot_general(
                part, high, dims, preferred_element_type=jnp.float32
            ) + lax.dot_general(part, low, dims, preferred_element_type=jnp.float32)


def whiten(text, tag, inverses, text_scale, tag_scale):
    return pl.pallas_call(
        functools.partial(white_kernel, text_scale, tag_scale),
        out_shape=(
            jax.ShapeDtypeStruct(text.shape, jnp.float32),
            jax.ShapeDtypeStruct(tag.shape, jnp.float32),
        ),
        in_specs=[pl.BlockSpec(memory_space=VMEM)] * 3,
        out_specs=[pl.BlockSpec(memory_space=VMEM)] * 2,
        compiler_params=pltpu.CompilerParams(vmem_limit_bytes=16 << 20),
    )(text, tag, inverses)


def local_gram(panel):
    return lax.dot_general(
        panel, panel, (((0,), (0,)), ((), ())), preferred_element_type=jnp.float32
    )


MESH = pl.DeviceIdType.MESH


def flip(me, offset):
    total, bit = me, 1
    while bit <= offset:
        if offset & bit:
            total = total + bit * (1 - 2 * lax.rem(lax.div(me, bit), 2))
        bit *= 2
    return total


def hypercube(size, rows, unit):
    bits = size.bit_length() - 1
    down = tuple(reversed(range(bits)))
    orders = [down]
    if bits >= 3:
        orders += [down[:-2] + (down[-1], down[-2]), (0, 1) + down[:-2]]
    units = rows // unit
    pieces, at = [], 0
    for number, order in enumerate(orders):
        here = units // len(orders) + (1 if number < units % len(orders) else 0)
        if here:
            pieces.append((order, at * unit, (at + here) * unit))
            at += here
    return pieces


def arrivals(order, stage):
    found = [1 << order[stage]]
    for bit in order[:stage]:
        found += [offset | 1 << bit for offset in found]
    return found


def greet(groups):
    barrier = pltpu.get_barrier_semaphore()
    for device in groups:
        pl.semaphore_signal(barrier, inc=1, device_id=device, device_id_type=MESH)
    pl.semaphore_wait(barrier, len(groups))


def tag_partners(size):
    me = lax.axis_index("tag")
    return [{"tag": flip(me, 1 << bit)} for bit in range(size.bit_length() - 1)]


def spread(pieces, source, place, send, recv):
    me = lax.axis_index("tag")
    copies = {}

    def go(number, offset, bit):
        order, lo, hi = pieces[number]
        owner = flip(me, offset)
        to = offset | 1 << bit
        copies[number, to] = pltpu.make_async_remote_copy(
            src_ref=source(lo, hi) if offset == 0 else place(owner, lo, hi),
            dst_ref=place(owner, lo, hi),
            send_sem=send.at[number, to],
            recv_sem=recv.at[number, to],
            device_id={"tag": flip(me, 1 << bit)},
            device_id_type=MESH,
        )
        copies[number, to].start()

    bits = len(pieces[0][0])
    for stage in range(bits):
        for number, (order, _, _) in enumerate(pieces):
            go(number, 0, order[stage])
    for stage in range(bits):
        for turn in range(1 << stage):
            for number, (order, _, _) in enumerate(pieces):
                offset = arrivals(order, stage)[turn]
                copies[number, offset].wait_recv()
                for later in range(stage + 1, bits):
                    go(number, offset, order[later])
    return copies


def collect_start(pieces, source, land, send, recv):
    me = lax.axis_index("tag")
    copies = {}
    last = len(pieces[0][0]) - 1
    for turn in range(1 << last):
        for number, (order, lo, hi) in enumerate(pieces):
            offset = arrivals(order, last)[turn]
            copies[number, offset] = pltpu.make_async_remote_copy(
                src_ref=source(flip(me, offset), lo, hi),
                dst_ref=land.at[offset, lo:hi],
                send_sem=send.at[number, offset],
                recv_sem=recv.at[number, offset],
                device_id={"tag": flip(me, 1 << order[last])},
                device_id_type=MESH,
            )
            copies[number, offset].start()
    return copies


def collect(pieces, copies, source, land, outgoing, finish, send, recv):
    me = lax.axis_index("tag")
    bits = len(pieces[0][0])

    def summed(number, offset, stage):
        order, lo, hi = pieces[number]
        total = source(flip(me, offset), lo, hi)[...].astype(jnp.float32)
        for later in reversed(range(stage + 1, bits)):
            come = offset | 1 << order[later]
            copies[number, come].wait_recv()
            total = total + land[come, lo:hi].astype(jnp.float32)
        return total

    for stage in reversed(range(bits - 1)):
        for turn in range(1 << stage):
            for number, (order, lo, hi) in enumerate(pieces):
                offset = arrivals(order, stage)[turn]
                outgoing[offset, lo:hi] = summed(number, offset, stage).astype(outgoing.dtype)
                copies[number, offset] = pltpu.make_async_remote_copy(
                    src_ref=outgoing.at[offset, lo:hi],
                    dst_ref=land.at[offset, lo:hi],
                    send_sem=send.at[number, offset],
                    recv_sem=recv.at[number, offset],
                    device_id={"tag": flip(me, 1 << order[stage])},
                    device_id_type=MESH,
                )
                copies[number, offset].start()
    for number, (_, lo, hi) in enumerate(pieces):
        finish(lo, hi, summed(number, 0, -1))


def drain(copies):
    for copy in copies.values():
        copy.wait_send()


def gather_kernel(size, pieces, shard, out, send, recv):
    rows = shard.shape[0]
    greet(tag_partners(size))

    def place(owner, lo, hi):
        return out.at[pl.ds(pl.multiple_of(owner * rows + lo, 16), hi - lo), :]

    copies = spread(pieces, lambda lo, hi: shard.at[lo:hi, :], place, send, recv)
    me = lax.axis_index("tag")
    out[pl.ds(pl.multiple_of(me * rows, 16), rows), :] = shard[...]
    drain(copies)


def remote_call(kernel, number, out_shape, scratch, count):
    many = isinstance(out_shape, tuple)
    spec = pl.BlockSpec(memory_space=VMEM)
    return pl.pallas_call(
        kernel,
        out_shape=out_shape,
        in_specs=[spec] * count,
        out_specs=[spec] * len(out_shape) if many else spec,
        scratch_shapes=scratch,
        cost_estimate=pl.CostEstimate(flops=0, bytes_accessed=50_000_000, transcendentals=0),
        compiler_params=pltpu.CompilerParams(
            collective_id=number, has_side_effects=True, vmem_limit_bytes=20 << 20
        ),
    )


def semaphores(*shape):
    return pltpu.SemaphoreType.DMA(shape)


def gather(shard, size):
    rows, comps = shard.shape
    pieces = hypercube(size, rows, 16)
    return remote_call(
        functools.partial(gather_kernel, size, pieces),
        0,
        jax.ShapeDtypeStruct((rows * size, comps), shard.dtype),
        [semaphores(len(pieces), size), semaphores(len(pieces), size)],
        1,
    )(shard)


def scatter_kernel(size, pieces, partial, out, land, outgoing, send, recv):
    rows = out.shape[0]
    greet(tag_partners(size))

    def source(owner, lo, hi):
        return partial.at[pl.ds(pl.multiple_of(owner * rows + lo, 16), hi - lo), :]

    def finish(lo, hi, total):
        out[lo:hi, :] = total.astype(out.dtype)

    copies = collect_start(pieces, source, land, send, recv)
    collect(pieces, copies, source, land, outgoing, finish, send, recv)
    drain(copies)


def scatter_sum(partial, size):
    rows, comps = partial.shape[0] // size, partial.shape[1]
    pieces = hypercube(size, rows, 16)
    return remote_call(
        functools.partial(scatter_kernel, size, pieces),
        2,
        jax.ShapeDtypeStruct((rows, comps), jnp.bfloat16),
        [
            VMEM((size, rows, comps), jnp.bfloat16),
            VMEM((size, rows, comps), jnp.bfloat16),
            semaphores(len(pieces), size),
            semaphores(len(pieces), size),
        ],
        1,
    )(partial)


def spread_steps(pieces, source, place, send, recv, copies):
    me = lax.axis_index("tag")

    def go(number, offset, bit):
        order, lo, hi = pieces[number]
        owner = flip(me, offset)
        to = offset | 1 << bit
        copies[number, to] = pltpu.make_async_remote_copy(
            src_ref=source(lo, hi) if offset == 0 else place(owner, lo, hi),
            dst_ref=place(owner, lo, hi),
            send_sem=send.at[number, to],
            recv_sem=recv.at[number, to],
            device_id={"tag": flip(me, 1 << bit)},
            device_id_type=MESH,
        )
        copies[number, to].start()

    bits = len(pieces[0][0])
    for stage in range(bits):
        for number, (order, _, _) in enumerate(pieces):
            go(number, 0, order[stage])
    yield
    for stage in range(bits):
        for turn in range(1 << stage):
            for number, (order, _, _) in enumerate(pieces):
                offset = arrivals(order, stage)[turn]
                copies[number, offset].wait_recv()
                for later in range(stage + 1, bits):
                    go(number, offset, order[later])
                yield number, offset


def collect_steps(pieces, source, land, outgoing, finish, send, recv, copies, before):
    me = lax.axis_index("tag")
    bits = len(pieces[0][0])

    def go(number, offset, bit, ref):
        _, lo, hi = pieces[number]
        copies[number, offset] = pltpu.make_async_remote_copy(
            src_ref=ref,
            dst_ref=land(offset, lo, hi),
            send_sem=send.at[number, offset],
            recv_sem=recv.at[number, offset],
            device_id={"tag": flip(me, 1 << bit)},
            device_id_type=MESH,
        )
        copies[number, offset].start()

    def summed(number, offset, stage):
        order, lo, hi = pieces[number]
        total = source(flip(me, offset), lo, hi)[...].astype(jnp.float32)
        for later in reversed(range(stage + 1, bits)):
            come = offset | 1 << order[later]
            copies[number, come].wait_recv()
            total = total + land(come, lo, hi)[...].astype(jnp.float32)
        return total

    last = bits - 1
    for turn in reversed(range(1 << last)):
        for number, (order, lo, hi) in enumerate(pieces):
            offset = arrivals(order, last)[turn]
            before(offset)
            go(number, offset, order[last], source(flip(me, offset), lo, hi))
    before(0)
    yield
    for stage in reversed(range(last)):
        for turn in reversed(range(1 << stage)):
            for number, (order, lo, hi) in enumerate(pieces):
                offset = arrivals(order, stage)[turn]
                leaving = outgoing(offset, lo, hi)
                leaving[...] = summed(number, offset, stage).astype(leaving.dtype)
                go(number, offset, order[stage], leaving)
                yield
    for number, (_, lo, hi) in enumerate(pieces):
        finish(lo, hi, summed(number, 0, -1))
        yield


def advance(steps, count):
    for _ in range(count):
        next(steps, None)


def finish_steps(steps):
    for _ in steps:
        pass


def front_kernel(
    size, pieces, shard, stored, tile_rows, tile_cols, tile_counts, text_out, tag_out, tag_gram,
    tiles, table, panel, total, leaving, arrived, columns, partial, land, outgoing,
    tile_sem, gather_sems, pair_sems, scatter_sems, *gram_refs,
):
    core = lax.axis_index("text")
    me = lax.axis_index("tag")
    sibling = {"text": 1 - core}
    slots, width, _ = stored.shape
    rows = shard.shape[0]
    row_span, column_span = panel.shape[0], columns.shape[0]
    row_tiles, column_tiles = row_span // width, column_span // width
    share = width // rows
    half = column_span // 2
    chunk = half // column_tiles
    load = pltpu.make_async_copy(stored, tiles.at[0:slots], tile_sem)
    load.start()
    greet(tag_partners(size) + [sibling])

    def place(owner, lo, hi):
        return panel.at[pl.ds(pl.multiple_of(owner * rows + lo, 16), hi - lo), :]

    def source(owner, lo, hi):
        return partial.at[pl.ds(pl.multiple_of(owner * rows + lo, 16), hi - lo), :]

    def row_tile(distance):
        return lax.div(flip(me, distance * share), share)

    def tile_rows_of(r):
        return pl.ds(pl.multiple_of(r * width, width), width)

    gathered, paired, summed = {}, {}, {}
    steps = spread_steps(
        pieces,
        lambda lo, hi: shard.at[lo:hi, :],
        place,
        gather_sems.at[0],
        gather_sems.at[1],
        gathered,
    )
    next(steps)
    tiles[slots] = jnp.zeros((width, width), tiles.dtype)
    for r in range(row_tiles):
        for c in range(column_tiles):
            found = jnp.int32(slots)
            for slot in range(slots):
                live = (tile_rows[0, slot] == r) & (tile_cols[0, slot] == c)
                found = jnp.where(live & (slot < tile_counts[0, 0]), slot, found)
            table[r * column_tiles + c] = found
    panel[pl.ds(pl.multiple_of(me * rows, 16), rows), :] = shard[...]

    def swap(phase, number, src, dst):
        copy = pltpu.make_async_remote_copy(
            src_ref=src,
            dst_ref=dst,
            send_sem=pair_sems.at[0, phase, number],
            recv_sem=pair_sems.at[1, phase, number],
            device_id=sibling,
            device_id_type=MESH,
        )
        copy.start()
        paired[phase, number] = copy

    finished = []

    def tag_products(distance):
        if not finished:
            load.wait()
        r = row_tile(distance)
        block = panel[tile_rows_of(r), :]
        sent = False
        for turn in range(column_tiles):
            c = core * turn + (1 - core) * (column_tiles - 1 - turn)
            product = lax.dot_general(
                tiles[table[r * column_tiles + c]],
                block,
                (((0,), (0,)), ((), ())),
                preferred_element_type=jnp.float32,
            )
            if not finished:
                total[tile_rows_of(c), :] = product
            else:
                total[tile_rows_of(c), :] += product
            if len(finished) == row_tiles - 1 and not sent and (turn + 1) * width >= half:
                sent = True
                for number in range(column_tiles):
                    lo = number * chunk
                    theirs = pl.ds(pl.multiple_of((1 - core) * half + lo, 16), chunk)
                    leaving[lo : lo + chunk, :] = total[theirs, :].astype(leaving.dtype)
                    swap(0, number, leaving.at[lo : lo + chunk, :], arrived.at[lo : lo + chunk, :])
        finished.append(distance)

    missing = {(number, offset) for number in range(len(pieces)) for offset in range(1, size)}
    for event in steps:
        missing.discard(event)
        waiting = {offset // share for _, offset in missing}
        for distance in range(row_tiles):
            if distance not in waiting and distance not in finished:
                tag_products(distance)

    for number in range(column_tiles):
        lo = number * chunk
        ours = pl.ds(pl.multiple_of(core * half + lo, 16), chunk)
        paired[0, number].wait_recv()
        value = total[ours, :] + arrived[lo : lo + chunk, :].astype(jnp.float32)
        value = value.astype(columns.dtype)
        columns[ours, :] = value
        tag_out[lo : lo + chunk, :] = value
        swap(1, number, columns.at[ours, :], columns.at[ours, :])
    for number in range(column_tiles):
        paired[1, number].wait_recv()

    grams = [{}, {}]
    both, mine, own, gram_land, gram_outgoing, gram_pair, gram_sems = gram_refs
    tag_steps = gram_steps(
        size, tag_out, both, mine, own, tag_gram, gram_land, gram_outgoing,
        gram_pair, gram_sems, grams,
    )
    next(tag_steps)
    ready = set()

    def text_products(offset):
        for distance in [offset // share] if offset else range(row_tiles):
            if distance in ready:
                continue
            ready.add(distance)
            r = row_tile(distance)
            value = None
            for c in range(column_tiles):
                product = jnp.dot(
                    tiles[table[r * column_tiles + c]],
                    columns[c * width : (c + 1) * width, :],
                    preferred_element_type=jnp.float32,
                )
                value = product if value is None else value + product
            partial[tile_rows_of(r), :] = value.astype(partial.dtype)
            advance(tag_steps, 6)

    def done(lo, hi, value):
        text_out[lo:hi, :] = value.astype(text_out.dtype)

    scatter_steps = collect_steps(
        pieces,
        source,
        lambda offset, lo, hi: land.at[offset, lo:hi, :],
        lambda offset, lo, hi: outgoing.at[offset, lo:hi, :],
        done,
        scatter_sems.at[0],
        scatter_sems.at[1],
        summed,
        text_products,
    )
    for _ in scatter_steps:
        advance(tag_steps, 2)
    finish_steps(tag_steps)
    for copies in (gathered, paired, summed, *grams):
        drain(copies)


def front(shard, tiles, tile_rows, tile_cols, tile_counts, size):
    rows, comps = shard.shape
    slots, width, _ = tiles.shape
    row_span, column_span = rows * size, TC * width
    half = column_span // 2
    blocks = len(lower(comps // LANES))
    pieces = hypercube(size, rows, 16)
    narrow = jnp.bfloat16
    vmem, smem = pl.BlockSpec(memory_space=VMEM), pl.BlockSpec(memory_space=pltpu.SMEM)
    return pl.pallas_call(
        functools.partial(front_kernel, size, pieces),
        out_shape=(
            jax.ShapeDtypeStruct((rows, comps), narrow),
            jax.ShapeDtypeStruct((half, comps), narrow),
            jax.ShapeDtypeStruct((blocks // 2, LANES, LANES), jnp.float32),
        ),
        in_specs=[vmem, pl.BlockSpec(memory_space=pltpu.HBM), smem, smem, smem],
        out_specs=[vmem, vmem, vmem],
        scratch_shapes=[
            VMEM((slots + 1, width, width), narrow),
            pltpu.SMEM((row_span // width * TC,), jnp.int32),
            VMEM((row_span, comps), narrow),
            VMEM((column_span, comps), jnp.float32),
            VMEM((half, comps), narrow),
            VMEM((half, comps), narrow),
            VMEM((column_span, comps), narrow),
            VMEM((row_span, comps), narrow),
            VMEM((size, rows, comps), narrow),
            VMEM((size, rows, comps), narrow),
            pltpu.SemaphoreType.DMA,
            semaphores(2, len(pieces), size),
            semaphores(2, 2, TC),
            semaphores(2, len(pieces), size),
            *gram_scratch(comps, size),
        ],
        cost_estimate=pl.CostEstimate(flops=0, bytes_accessed=50_000_000, transcendentals=0),
        compiler_params=pltpu.CompilerParams(
            collective_id=5, has_side_effects=True, vmem_limit_bytes=52 << 20
        ),
    )(shard, tiles, tile_rows, tile_cols, tile_counts)


def lower(blocks):
    return [(i, j) for i in range(blocks) for j in range(i + 1)]


def gram_steps(size, panel, both, mine, own, gathered, land, outgoing, pair, sems, copies):
    core = lax.axis_index("text")
    me = lax.axis_index("tag")
    rows = own.shape[1]
    share = mine.shape[0]
    pieces = hypercube(size, share, 1)
    gram = local_gram(panel[...])
    for at, (i, j) in enumerate(lower(gram.shape[0] // LANES)):
        both[at] = gram[i * LANES : (i + 1) * LANES, j * LANES : (j + 1) * LANES]
    swap = pltpu.make_async_remote_copy(
        src_ref=both.at[pl.ds((1 - core) * share, share)],
        dst_ref=mine,
        send_sem=pair.at[0],
        recv_sem=pair.at[1],
        device_id={"text": 1 - core},
        device_id_type=MESH,
    )
    swap.start()
    yield
    swap.wait()
    mine[...] += both[pl.ds(core * share, share)]

    def place(owner, lo, hi):
        return gathered.at[lo:hi, pl.ds(pl.multiple_of(owner * rows, 8), rows), :]

    def source(owner, lo, hi):
        return mine.at[lo:hi, pl.ds(pl.multiple_of(owner * rows, 8), rows), :]

    def finish(lo, hi, total):
        own[lo:hi] = total

    yield from collect_steps(
        pieces,
        source,
        lambda offset, lo, hi: land.at[offset, lo:hi],
        lambda offset, lo, hi: outgoing.at[offset, lo:hi],
        finish,
        sems.at[0],
        sems.at[1],
        copies[0],
        lambda offset: None,
    )
    yield from spread_steps(
        pieces, lambda lo, hi: own.at[lo:hi], place, sems.at[2], sems.at[3], copies[1]
    )
    gathered[:, pl.ds(pl.multiple_of(me * rows, 8), rows), :] = own[...]


def gram_scratch(comps, size):
    count = len(lower(comps // LANES))
    share, rows = count // 2, LANES // size
    pieces = hypercube(size, share, 1)
    return [
        VMEM((count, LANES, LANES), jnp.float32),
        VMEM((share, LANES, LANES), jnp.float32),
        VMEM((share, rows, LANES), jnp.float32),
        VMEM((size, share, rows, LANES), jnp.float32),
        VMEM((size, share, rows, LANES), jnp.float32),
        semaphores(2),
        semaphores(4, len(pieces), size),
    ]


def gram_kernel(
    size, text, tag, out, halves, whole, both, mine, own, land, outgoing, pair, sems, last
):
    core = lax.axis_index("text")
    sibling = {"text": 1 - core}
    share = tag.shape[0]
    greet(tag_partners(size) + [sibling])
    copies = [{}, {}]
    finish_steps(
        gram_steps(
            size, text, both, mine, own, halves.at[0], land, outgoing, pair, sems, copies
        )
    )
    halves[1] = tag[...]
    swap = pltpu.make_async_remote_copy(
        src_ref=halves.at[1 - core],
        dst_ref=whole.at[pl.ds(core * share, share)],
        send_sem=last.at[0],
        recv_sem=last.at[1],
        device_id=sibling,
        device_id_type=MESH,
    )
    swap.start()
    whole[pl.ds(core * share, share)] = halves[core]
    swap.wait()
    for group in copies:
        drain(group)
    for at, (i, j) in enumerate(lower(out.shape[0] // LANES)):
        block = whole[at]
        if i != j:
            out[j * LANES : (j + 1) * LANES, i * LANES : (i + 1) * LANES] = block.T
        out[i * LANES : (i + 1) * LANES, j * LANES : (j + 1) * LANES] = block


def gram_sum(text, tag, size):
    comps = text.shape[1]
    share = tag.shape[0]
    return remote_call(
        functools.partial(gram_kernel, size),
        3,
        jax.ShapeDtypeStruct((comps, comps), jnp.float32),
        [
            VMEM((2, share, LANES, LANES), jnp.float32),
            VMEM((2 * share, LANES, LANES), jnp.float32),
            *gram_scratch(comps, size),
            semaphores(2),
        ],
        2,
    )(text, tag)


def factor_swap_kernel(gram, out, work, scale, sems):
    core = lax.axis_index("text")
    sibling = {"text": 1 - core}
    greet([sibling])
    copies = []

    def store(lo, hi, value):
        out[core, lo:hi, :] = value
        copy = pltpu.make_async_remote_copy(
            src_ref=out.at[core, lo:hi, :],
            dst_ref=out.at[core, lo:hi, :],
            send_sem=sems.at[0, len(copies)],
            recv_sem=sems.at[1, len(copies)],
            device_id=sibling,
            device_id_type=MESH,
        )
        copy.start()
        copies.append(copy)

    work[...] = gram[...]
    factor_in_place(work, scale, store)
    for copy in copies:
        copy.wait()


def inverse_factors(gram):
    return remote_call(
        factor_swap_kernel,
        4,
        jax.ShapeDtypeStruct((2,) + gram.shape, jnp.float32),
        [
            VMEM(gram.shape, jnp.float32),
            VMEM((1, gram.shape[1]), jnp.float32),
            semaphores(2, gram.shape[0] // LANES),
        ],
        1,
    )(gram)


def shards(tile_values, tile_rows, tile_cols, tile_counts, panel_init):
    tiles = tile_values[0]
    rows = tile_rows[0]
    cols = tile_cols[0]
    count = tile_counts[0]
    width = tiles.shape[1]
    comps = panel_init.shape[1]
    text_size = lax.axis_size("text")
    tag_size = lax.axis_size("tag")
    column_span = TC * width
    share = column_span // text_size
    blocks = len(lower(comps // LANES))
    paired = text_size == 2 and LANES // tag_size >= 8 and blocks % 2 == 0
    if paired:
        text_mine, tag_mine, tag_gram = front(
            panel_init, tiles, tile_rows, tile_cols, tile_counts, tag_size
        )
    else:
        row_block = gather(panel_init, tag_size)
        row_span = row_block.shape[0]
        tag_partial = tile_product(
            tag_kernel, tiles, rows, cols, count, row_block, column_span, jnp.float32, []
        )
        column_block = lax.psum(tag_partial, "text").astype(jnp.bfloat16)
        tag_mine = lax.dynamic_slice_in_dim(
            column_block, lax.axis_index("text") * share, share, 0
        )
        text_partial = tile_product(
            text_kernel,
            tiles,
            rows,
            cols,
            count,
            column_block,
            row_span,
            jnp.bfloat16,
            [VMEM((row_span, comps), jnp.float32)],
        )
        text_mine = scatter_sum(text_partial, tag_size)
    if paired:
        inverses = inverse_factors(gram_sum(text_mine, tag_gram, tag_size))
    else:
        text_gram, tag_gram = lax.psum(
            (local_gram(text_mine), local_gram(tag_mine)), ("text", "tag")
        )
        inverses = jnp.stack([inverse_factor(text_gram), inverse_factor(tag_gram)])
    text_total = text_mine.shape[0] * tag_size * text_size
    tag_total = column_span * tag_size
    return whiten(text_mine, tag_mine, inverses, math.sqrt(text_total), math.sqrt(tag_total))


def solution(mesh):
    in_specs = (
        P("text", "tag", None, None),
        P("text", "tag"),
        P("text", "tag"),
        P("text", "tag"),
        P(("text", "tag"), None),
    )
    out_specs = (P(("text", "tag"), None), P(("tag", "text"), None))
    return jax.shard_map(shards, mesh=mesh, in_specs=in_specs, out_specs=out_specs, check_vma=False)
```
